512 devices in a mesh: hi: 16 (over z, y_hi), lo: 32 (over x, y_lo, core).
Axes of the slice: x: 4, y: 8 (y_hi: 2, y_lo: 4; y = y_hi * 4 + y_lo), z: 8, core: 2. Of those that a mesh axis runs over, the one named last changes fastest.
Arguments:
- amplitudes: float32 [16, 32, 32, 128, 128], P('hi', 'lo'), may hold values from -6 to 6
- gates: float32 [3, 128, 128], replicated, may hold values from -0.5 to 0.5
- angles: float32 [2], replicated, may hold values from -3.140625 to 3.140625
- cz_pairs: int32 [24, 2], replicated, may hold values from 0 to 18, as said below
Outputs:
- rotated: float32 [16, 32, 32, 128, 128], P('hi', 'lo')
The draws below stay inside these ranges and needn't reach their ends.
Inputs may be any that keep to these rules, and one draw needn't show every extreme that they name: `cz_pairs`: the two qubits of a row differ.
All inputs are finite; a program needn't handle non-finite values.
Results may differ from the reference program's by a relative error of at most 0.00007.
Values sent between devices are 32-bit elements; how exact they have to be, the bound alone decides.
No kernel may reach another device: no remote copies, remote signals or barrier semaphores. Data moves between devices by JAX's collectives and lax.ppermute only.
A program may use at most 64 MiB of HBM per device.

```python
import jax
import jax.numpy as jnp
from jax import lax

QG = 7
GATE = 128
QM = 5
MID = 32
NCZ = 24
N_HI = 16
N_LO = 32


def draw_cz_pairs(key, part):
    qubits = 2 * QG + QM
    key_first, key_step = jax.random.split(jax.random.fold_in(key, 17))
    first_qubit = jax.random.randint(key_first, (NCZ,), 0, qubits, dtype=jnp.int32)
    step_size = jax.random.randint(key_step, (NCZ,), 1, qubits, dtype=jnp.int32)
    second_qubit = (first_qubit + step_size) % qubits
    first_qubit = first_qubit.at[0].set(0)
    second_qubit = second_qubit.at[0].set(qubits - 1)
    return jnp.stack((first_qubit, second_qubit), 1)


def level_of(key, dims, shards, low, top_value):
    def one(dim, shards_of):
        steps = jax.random.uniform(jax.random.fold_in(jax.random.fold_in(key, 6), dim), (shards_of,), jnp.float32, low / len(shards), top_value / len(shards))
        return jnp.repeat(jnp.exp(steps), dims[dim] // shards_of).reshape((-1,) + (1,) * (len(dims) - dim - 1))

    level = one(*shards[0])
    for cut in shards[1:]:
        level = level * one(*cut)
    return level


def noise(stream_key, dims, width, most, cuts=(), kind=jnp.bfloat16):
    values = jax.random.normal(stream_key, dims, jnp.float32) * width
    if len(cuts) > 0:
        values = level_of(stream_key, dims, cuts, -0.22, 0.18) * values
    return jnp.clip(values, min=-most, max=most).astype(kind)


def setup_inputs(seed: int = 0) -> dict:
    key_of = jax.random.split(jax.random.key(seed), 5)
    return {
        "amplitudes": noise(key_of[0], (N_HI, N_LO, MID, GATE, GATE), 1.0, 6.0, ((0, 16), (1, 32)), jnp.float32),
        "gates": noise(key_of[1], (3, GATE, GATE), GATE ** -0.5, 0.5, (), jnp.float32),
        "angles": jnp.clip(jax.random.uniform(key_of[2], (2,), jnp.float32, -3.140625, 3.140625), -3.140625, 3.140625),
        "cz_pairs": draw_cz_pairs(jax.random.fold_in(key_of[4], 71), 0),
    }


def group_bits(qubit_index, offset, bit_count):
    inside = ((qubit_index >= offset) & (qubit_index < offset + bit_count)).astype(jnp.int32)
    shifted = jnp.clip(qubit_index - offset, 0, bit_count - 1).astype(jnp.int32)
    positions = jnp.arange(2 ** bit_count, dtype=jnp.int32)
    return ((positions[None, :] >> shifted[:, None]) & 1) * inside[:, None]


def parity_sign(values):
    return 1.0 - 2.0 * (values % 2).astype(jnp.float32)


def cross_table(left_a, right_b, left_b, right_a):
    return jnp.einsum('pi,pj->ij', left_a, right_b) + jnp.einsum('pi,pj->ij', left_b, right_a)


def cz_sign(cz_pairs):
    first_qubit = cz_pairs[:, 0].astype(jnp.int32)
    second_qubit = cz_pairs[:, 1].astype(jnp.int32)
    upper_a = group_bits(first_qubit, 2 * QG, QM)
    middle_a = group_bits(first_qubit, QG, QG)
    lowest_a = group_bits(first_qubit, 0, QG)
    upper_b = group_bits(second_qubit, 2 * QG, QM)
    middle_b = group_bits(second_qubit, QG, QG)
    lowest_b = group_bits(second_qubit, 0, QG)
    sign_um = parity_sign(cross_table(upper_a, middle_b, upper_b, middle_a))
    sign_ul = parity_sign(cross_table(upper_a, lowest_b, upper_b, lowest_a))
    sign_ml = parity_sign(cross_table(middle_a, lowest_b, middle_b, lowest_a))
    diag_u = parity_sign(jnp.sum(upper_a * upper_b, 0))
    diag_m = parity_sign(jnp.sum(middle_a * middle_b, 0))
    diag_l = parity_sign(jnp.sum(lowest_a * lowest_b, 0))
    left_table = sign_um * diag_u[:, None]
    right_table = sign_ml * diag_m[:, None] * diag_l[None, :]
    return left_table[:, :, None] * sign_ul[:, None, :] * right_table[None]


def rotate_pair(lower_half, upper_half, angle):
    cosine = jnp.cos(angle * 0.5)
    sine = jnp.sin(angle * 0.5)
    return cosine * lower_half - sine * upper_half, sine * lower_half + cosine * upper_half


def reference(amplitudes, gates, angles, cz_pairs):
    hi_count, lo_count, mid_size, gate_size = amplitudes.shape[0], amplitudes.shape[1], amplitudes.shape[2], amplitudes.shape[4]
    full_shape = amplitudes.shape
    vector = amplitudes * cz_sign(cz_pairs)[None, None]
    vector = jnp.einsum('hlmjc,kc->hlmjk', vector, gates[0], precision=lax.Precision.HIGHEST)
    paired = vector.reshape(hi_count, 2, lo_count // 2, mid_size, gate_size, gate_size)
    lower_half, upper_half = rotate_pair(paired[:, 0], paired[:, 1], angles[0])
    vector = jnp.stack((lower_half, upper_half), 1).reshape(full_shape)
    vector = jnp.einsum('jc,hlmck->hlmjk', gates[1], vector, precision=lax.Precision.HIGHEST)
    paired = vector.reshape(hi_count // 2, 2, lo_count, mid_size, gate_size, gate_size)
    lower_half, upper_half = rotate_pair(paired[:, 0], paired[:, 1], angles[1])
    vector = jnp.stack((lower_half, upper_half), 1).reshape(full_shape)
    vector = vector.reshape(hi_count, lo_count, hi_count, mid_size // hi_count, gate_size, gate_size)
    vector = jnp.swapaxes(vector, 0, 2).reshape(hi_count, lo_count, gate_size, mid_size * gate_size)
    vector = jnp.einsum('ic,hlcn->hlin', gates[2], vector, precision=lax.Precision.HIGHEST)
    return vector.reshape(full_shape)
```

```python
import jax
import jax.numpy as jnp
from jax import lax
from jax.experimental import pallas as pl
from jax.experimental.pallas import tpu as pltpu
from jax.sharding import PartitionSpec as P

QL = 14
QU = 5
QUBITS = QL + QU
PARTS = 2


def split(value):
    top = value.astype(jnp.bfloat16)
    return top, (value - top.astype(jnp.float32)).astype(jnp.bfloat16)


def fold_parity(bits):
    for step in (8, 4, 2, 1):
        bits = bits ^ (bits >> step)
    return bits & 1


def mm(left, right):
    return lax.dot_general(left, right, (((1,), (0,)), ((), ())), preferred_element_type=jnp.float32)


def local_kernel(step_t, cz_ref, x_ref, g_ref, *rest):
    outs = rest[:PARTS]
    adj, masks, flips, low_sign, right0, left1 = rest[PARTS:]
    step = pl.program_id(0)

    @pl.when(step == 0)
    def _():
        for q in range(QUBITS):
            adj[q] = 0
        for p in range(cz_ref.shape[0]):
            a = cz_ref[p, 0]
            b = cz_ref[p, 1]
            q = jnp.maximum(a, b)
            adj[q] = adj[q] ^ (1 << jnp.minimum(a, b))
        masks[0] = 0
        flips[0] = 0
        for u in range(QU):
            row = adj[QL + u]
            for m in range(1 << u):
                masks[m + (1 << u)] = masks[m] ^ (row & ((1 << QL) - 1))
                flips[m + (1 << u)] = flips[m] ^ fold_parity((row >> QL) & m)
        row_id = lax.broadcasted_iota(jnp.int32, (128, 128), 0)
        lane_id = lax.broadcasted_iota(jnp.int32, (128, 128), 1)
        index = row_id * 128 + lane_id
        partner = jnp.zeros_like(index)
        for q in range(1, QL):
            partner = partner ^ jnp.where((index >> q & 1) == 1, adj[q], 0)
        low_sign[...] = 1.0 - 2.0 * fold_parity(index & partner).astype(jnp.float32)
        hi0, lo0 = split(g_ref[0].T)
        right0[0:128, 0:128] = hi0
        right0[0:128, 128:256] = lo0
        right0[128:256, 0:128] = hi0
        right0[128:256, 128:256] = jnp.zeros((128, 128), jnp.bfloat16)
        hi1, lo1 = split(g_ref[1])
        row = lax.broadcasted_iota(jnp.int32, (256, 128), 0)
        column = lax.broadcasted_iota(jnp.int32, (256, 128), 1)
        choose = jnp.where(column == (row & 3) * 32 + (row >> 3), 1.0, 0.0).astype(jnp.bfloat16)
        first = (row >> 2 & 1) == 0
        for i, part in enumerate((hi1, lo1)):
            picked = mm(choose, part)
            left1[i, :, 0:128] = jnp.where(first, picked, 0.0).astype(jnp.bfloat16)
            left1[i, :, 128:256] = jnp.where(first, 0.0, picked).astype(jnp.bfloat16)

    small = lax.broadcasted_iota(jnp.int32, (8, 128), 0) * 128 + lax.broadcasted_iota(jnp.int32, (8, 128), 1)
    for t in range(0, step_t, 2):
        tops = []
        lows = []
        for i in range(2):
            signed = []
            for r in range(2):
                m = (step * step_t + t + i) * 2 + r
                mask = masks[m]
                sign = 1.0 - 2.0 * (fold_parity(small & mask) ^ flips[m]).astype(jnp.float32)
                for q in range(10, QL):
                    flip = 1.0 - 2.0 * (mask >> q & 1).astype(jnp.float32)
                    sign = jnp.concatenate((sign, sign * flip), 0)
                signed.append(x_ref[t + i, r] * sign * low_sign[...])
            top, low = split(jnp.concatenate(signed, 0))
            both = mm(jnp.concatenate((top, low), 1), right0[...])
            top, low = split(both[:, 0:128] + both[:, 128:256])
            tops.append(top)
            lows.append(low)
        upper = jnp.concatenate(tops, 1)
        wide = mm(left1[0], jnp.concatenate((upper, *lows), 1))
        result = wide[:, 0:256] + wide[:, 256:512] + mm(left1[1], upper)
        size = 256 // PARTS
        for i in range(2):
            for c in range(PARTS):
                outs[c][t + i] = result[c * size : (c + 1) * size, i * 128 : (i + 1) * 128].reshape(size // 8, 8, 128)


def local_gates(x, gates, cz_pairs):
    step_t = 4
    part = jax.ShapeDtypeStruct((16, 32 // PARTS, 8, 128), jnp.float32)
    return pl.pallas_call(
        lambda *refs: local_kernel(step_t, *refs),
        out_shape=[part] * PARTS,
        grid=(16 // step_t,),
        in_specs=[
            pl.BlockSpec(memory_space=pltpu.SMEM),
            pl.BlockSpec((step_t, 2, 128, 128), lambda i: (i, 0, 0, 0)),
            pl.BlockSpec((3, 128, 128), lambda i: (0, 0, 0)),
        ],
        out_specs=[pl.BlockSpec((step_t, 32 // PARTS, 8, 128), lambda i: (i, 0, 0, 0))] * PARTS,
        scratch_shapes=[
            pltpu.SMEM((QUBITS,), jnp.int32),
            pltpu.SMEM((1 << QU,), jnp.int32),
            pltpu.SMEM((1 << QU,), jnp.int32),
            pltpu.VMEM((128, 128), jnp.float32),
            pltpu.VMEM((256, 256), jnp.bfloat16),
            pltpu.VMEM((2, 256, 256), jnp.bfloat16),
        ],
        name="local_gates",
    )(cz_pairs, x, gates)


def row_kernel(count, has_partner, has_base, *refs):
    turn_ref, g_ref = refs[:2]
    own_ref = refs[2]
    partner_ref = refs[3] if has_partner else None
    out_ref, left, right, lines = refs[3 + has_partner + has_base :]

    @pl.when(pl.program_id(0) == 0)
    def _():
        gate = g_ref[0]
        lane = lax.broadcasted_iota(jnp.int32, (128, 128), 1)
        odd = (lane >> 3 & 1) == 1
        crossed = jnp.where(odd, pltpu.roll(gate, 8, 1), pltpu.roll(gate, 120, 1))
        turned = turn_ref[2] * gate + jnp.where(odd, -turn_ref[3], turn_ref[3]) * crossed
        top, low = split(turned)
        left[:, 0:128] = top
        left[:, 128:256] = top
        left[:, 256:384] = low

    for s in range(8):
        value = own_ref[:, s].reshape(128, 128)
        if has_partner:
            value = turn_ref[0] * value + turn_ref[1] * partner_ref[:, s].reshape(128, 128)
        top, low = split(value)
        right[0:128, s * 128 : (s + 1) * 128] = top
        right[128:256, s * 128 : (s + 1) * 128] = low
    result = mm(left[:, 0:256], right[...]) + mm(left[:, 256:384], right[0:128, :])
    for s in range(8):
        lines[pl.ds(s, 128, stride=8), :] = result[:, s * 128 : (s + 1) * 128]
    out_ref[...] = lines[...].reshape(128, 1, 8, 128)


def row_gate(turn, gates, own, partner, base, first_group):
    groups = own.shape[1] // 8
    block = pl.BlockSpec((16, 8, 8, 128), lambda i: (0, i, 0, 0))
    operands = [turn, gates, own]
    specs = [
        pl.BlockSpec(memory_space=pltpu.SMEM),
        pl.BlockSpec((1, 128, 128), lambda i: (2, 0, 0)),
        block,
    ]
    if partner is not None:
        operands.append(partner)
        specs.append(block)
    aliases = {}
    if base is not None:
        aliases = {len(operands): 0}
        operands.append(base)
        specs.append(pl.BlockSpec(memory_space=pl.ANY))
    return pl.pallas_call(
        lambda *refs: row_kernel(groups, partner is not None, base is not None, *refs),
        out_shape=jax.ShapeDtypeStruct((128, 4, 8, 128), jnp.float32),
        grid=(groups,),
        in_specs=specs,
        out_specs=pl.BlockSpec((128, 1, 8, 128), lambda i: (0, first_group + i, 0, 0)),
        scratch_shapes=[
            pltpu.VMEM((128, 384), jnp.bfloat16),
            pltpu.VMEM((256, 1024), jnp.bfloat16),
            pltpu.VMEM((1024, 128), jnp.float32),
        ],
        input_output_aliases=aliases,
        name="row_gate",
    )(*operands)


def swap_lo(value, bit):
    return lax.ppermute(value, "lo", [(i, i ^ 1 << bit) for i in range(lax.axis_size("lo"))])


def remap(value):
    return lax.all_to_all(value, "hi", split_axis=0, concat_axis=0, tiled=True)


def per_device(amplitudes, gates, angles, cz_pairs):
    bit = lax.axis_size("lo").bit_length() - 2
    upper = (lax.axis_index("lo") >> bit & 1).astype(jnp.float32)
    cosines = jnp.cos(angles * 0.5)
    sines = jnp.sin(angles * 0.5)
    turn = jnp.stack((cosines[0], (2.0 * upper - 1.0) * sines[0], cosines[1], sines[1]))
    early, late = local_gates(amplitudes.reshape(16, 2, 128, 128), gates, cz_pairs)
    early_partner = swap_lo(early, bit)
    late = remap(late)
    late_partner = swap_lo(late, bit)
    early = remap(turn[0] * early + turn[1] * early_partner)
    result = row_gate(turn, gates, early, None, None, 0)
    result = row_gate(turn, gates, late, late_partner, result, 2)
    return result.reshape(amplitudes.shape)


def solution(mesh):
    placed = (P("hi", "lo", None, None, None), P(), P(), P())
    return jax.shard_map(
        per_device,
        mesh=mesh,
        in_specs=placed,
        out_specs=P("hi", "lo", None, None, None),
        check_vma=False,
    )
```

```python
import jax
import jax.numpy as jnp
from jax import lax
from jax.experimental import pallas as pl
from jax.experimental.pallas import tpu as pltpu
from jax.sharding import PartitionSpec as P

QL = 14
QU = 5
QUBITS = QL + QU
STEP = 2
SMEM = pl.BlockSpec(memory_space=pltpu.SMEM)
VMEM = pl.BlockSpec(memory_space=pltpu.VMEM)
ANY = pl.BlockSpec(memory_space=pl.ANY)
BOTH = (8, 2, 16, 8, 128)
ONE = (8, 16, 8, 128)


def split(value):
    top = value.astype(jnp.bfloat16)
    return top, (value - top.astype(jnp.float32)).astype(jnp.bfloat16)


def fold_parity(bits):
    for step in (8, 4, 2, 1):
        bits = bits ^ (bits >> step)
    return bits & 1


def mm(left, right):
    return lax.dot_general(left, right, (((1,), (0,)), ((), ())), preferred_element_type=jnp.float32)


def on_chip(value):
    return pltpu.with_memory_space_constraint(value, pltpu.VMEM)


def off_chip(value):
    return pltpu.with_memory_space_constraint(value, pltpu.HBM)


def gate_pair(left, upper, lower):
    wide = mm(left[0], jnp.concatenate((upper, lower), 1))
    return wide[:, 0:256] + wide[:, 256:512] + mm(left[1], upper)


def local_kernel(cz_ref, hi_ref, x_ref, g_ref, *rest):
    keep_ref, send_ref, upper_ref, lower_ref, late_left_ref = rest[:5]
    adj, masks, flips, low_sign, right0, left1 = rest[5:]
    step = pl.program_id(0)
    odd = hi_ref[0] & 1

    @pl.when(step == 0)
    def _():
        for q in range(QUBITS):
            adj[q] = 0
        for p in range(cz_ref.shape[1]):
            a = cz_ref[0, p]
            b = cz_ref[1, p]
            q = jnp.maximum(a, b)
            adj[q] = adj[q] ^ (1 << jnp.minimum(a, b))
        masks[0] = 0
        flips[0] = 0
        for u in range(QU):
            row = adj[QL + u]
            for m in range(1 << u):
                masks[m + (1 << u)] = masks[m] ^ (row & ((1 << QL) - 1))
                flips[m + (1 << u)] = flips[m] ^ fold_parity((row >> QL) & m)
        row_id = lax.broadcasted_iota(jnp.int32, (128, 128), 0)
        lane_id = lax.broadcasted_iota(jnp.int32, (128, 128), 1)
        index = row_id * 128 + lane_id
        partner = jnp.zeros_like(index)
        for q in range(1, QL):
            partner = partner ^ jnp.where((index >> q & 1) == 1, adj[q], 0)
        low_sign[...] = 1.0 - 2.0 * fold_parity(index & partner).astype(jnp.float32)
        hi0, lo0 = split(g_ref[0].T)
        right0[0:128, 0:128] = hi0
        right0[0:128, 128:256] = lo0
        right0[128:256, 0:128] = hi0
        right0[128:256, 128:256] = jnp.zeros((128, 128), jnp.bfloat16)
        hi1, lo1 = split(g_ref[1])
        row = lax.broadcasted_iota(jnp.int32, (256, 128), 0)
        column = lax.broadcasted_iota(jnp.int32, (256, 128), 1)
        choose = jnp.where(column == (row & 3) * 32 + (row >> 3), 1.0, 0.0).astype(jnp.bfloat16)
        first = (row >> 2 & 1) == 0
        for i, part in enumerate((hi1, lo1)):
            picked = mm(choose, part)
            one = jnp.where(first, picked, 0.0).astype(jnp.bfloat16)
            other = jnp.where(first, 0.0, picked).astype(jnp.bfloat16)
            left1[i, :, 0:128] = one[0:128]
            left1[i, :, 128:256] = other[0:128]
            late_left_ref[i, :, 0:128] = one[128:256]
            late_left_ref[i, :, 128:256] = other[128:256]

    small = lax.broadcasted_iota(jnp.int32, (8, 128), 0) * 128 + lax.broadcasted_iota(jnp.int32, (8, 128), 1)
    for local in range(STEP):
        z = step * STEP + local
        tops = []
        lows = []
        for s in range(2):
            signed = []
            y = odd ^ s
            for r in range(2):
                m = z * 4 + y * 2 + r
                mask = masks[m]
                sign = 1.0 - 2.0 * (fold_parity(small & mask) ^ flips[m]).astype(jnp.float32)
                for q in range(10, QL):
                    flip = 1.0 - 2.0 * (mask >> q & 1).astype(jnp.float32)
                    sign = jnp.concatenate((sign, sign * flip), 0)
                signed.append(x_ref[local, y, r] * sign * low_sign[...])
            top, low = split(jnp.concatenate(signed, 0))
            both = mm(jnp.concatenate((top, low), 1), right0[...])
            top, low = split(both[:, 0:128] + both[:, 128:256])
            tops.append(top)
            lows.append(low)
        upper = jnp.concatenate(tops, 1)
        lower = jnp.concatenate(lows, 1)
        upper_ref[z] = upper
        lower_ref[z] = lower
        result = gate_pair(left1, upper, lower)
        keep_ref[z] = result[:, 0:128].reshape(16, 8, 128)
        send_ref[z] = result[:, 128:256].reshape(16, 8, 128)


def local_gates(x, gates, cz_pairs, hi):
    held = pltpu.VMEM((8, 256, 256), jnp.bfloat16)
    return pl.pallas_call(
        local_kernel,
        out_shape=[
            pltpu.VMEM(ONE, jnp.float32),
            pltpu.VMEM(ONE, jnp.float32),
            held,
            held,
            pltpu.VMEM((2, 128, 256), jnp.bfloat16),
        ],
        grid=(8 // STEP,),
        in_specs=[
            SMEM,
            SMEM,
            pl.BlockSpec((STEP, 2, 2, 128, 128), lambda i: (i, 0, 0, 0, 0)),
            pl.BlockSpec((3, 128, 128), lambda i: (0, 0, 0)),
        ],
        out_specs=[VMEM] * 5,
        scratch_shapes=[
            pltpu.SMEM((QUBITS,), jnp.int32),
            pltpu.SMEM((1 << QU,), jnp.int32),
            pltpu.SMEM((1 << QU,), jnp.int32),
            pltpu.VMEM((128, 128), jnp.float32),
            pltpu.VMEM((256, 256), jnp.bfloat16),
            pltpu.VMEM((2, 128, 256), jnp.bfloat16),
        ],
        compiler_params=pltpu.CompilerParams(vmem_limit_bytes=16 << 20),
        name="local_gates",
    )(cz_pairs.T, hi, off_chip(x), off_chip(gates))


def late_kernel(upper_ref, lower_ref, left_ref, late_ref):
    for i in range(STEP):
        z = pl.program_id(0) * STEP + i
        result = gate_pair(left_ref, upper_ref[z], lower_ref[z])
        for s in range(2):
            late_ref[i, s] = result[:, s * 128 : (s + 1) * 128].reshape(16, 8, 128)


def late_gate(upper, lower, left):
    return pl.pallas_call(
        late_kernel,
        out_shape=jax.ShapeDtypeStruct(BOTH, jnp.float32),
        grid=(8 // STEP,),
        in_specs=[VMEM] * 3,
        out_specs=pl.BlockSpec((STEP, 2, 16, 8, 128), lambda i: (i, 0, 0, 0, 0)),
        compiler_params=pltpu.CompilerParams(vmem_limit_bytes=6 << 20),
        name="late_gate",
    )(on_chip(upper), on_chip(lower), on_chip(left))


def lo_turn(cos_ref, sin_ref, lo_ref):
    sine = sin_ref[0]
    return cos_ref[0], jnp.where((lo_ref[0] >> 4 & 1) == 1, sine, -sine)


def merge_kernel(cos_ref, sin_ref, lo_ref, keep, keep_partner, other, other_partner, late_keep, out_ref):
    c, f = lo_turn(cos_ref, sin_ref, lo_ref)
    part = pl.ds(pl.program_id(0) * STEP, STEP)
    out_ref[:, 0] = c * keep[part] + f * keep_partner[part]
    out_ref[:, 1] = c * other[part] + f * other_partner[part]


def merge(turn, parts, late_keep):
    return pl.pallas_call(
        merge_kernel,
        out_shape=jax.ShapeDtypeStruct(BOTH, jnp.float32),
        grid=(8 // STEP,),
        in_specs=[SMEM] * 3 + [VMEM] * 5,
        out_specs=pl.BlockSpec((STEP, 2, 16, 8, 128), lambda i: (i, 0, 0, 0, 0)),
        compiler_params=pltpu.CompilerParams(vmem_limit_bytes=6 << 20),
        name="merge",
    )(*turn, *map(on_chip, parts), on_chip(late_keep))


def cut_kernel(in_ref, left_ref, keep_ref, send_ref):
    keep_ref[...] = in_ref[:, 0]
    send_ref[...] = in_ref[:, 1]


def cut(value, left):
    return pl.pallas_call(
        cut_kernel,
        out_shape=[pltpu.VMEM(ONE, jnp.float32)] * 2,
        in_specs=[VMEM, VMEM],
        out_specs=[VMEM] * 2,
        compiler_params=pltpu.CompilerParams(vmem_limit_bytes=4 << 20),
        name="cut",
    )(on_chip(value), on_chip(left))


def matrix_kernel(cos_ref, sin_ref, hi_ref, g_ref, keep_partner, other, left_ref):
    gate = g_ref[0]
    lane = lax.broadcasted_iota(jnp.int32, (128, 128), 1)
    upper = (lane >> 3 & 1) == 1
    crossed = jnp.where(upper, pltpu.roll(gate, 8, 1), pltpu.roll(gate, 120, 1))
    cosine = cos_ref[1]
    sine = jnp.where(upper, -sin_ref[1], sin_ref[1])
    turned = jnp.where((hi_ref[0] & 1) == 1, cosine * crossed - sine * gate, cosine * gate + sine * crossed)
    top, low = split(turned)
    left_ref[:, 0:128] = top
    left_ref[:, 128:256] = top
    left_ref[:, 256:384] = low


def row_matrix(cosines, sines, hi, gates, *after):
    return pl.pallas_call(
        matrix_kernel,
        out_shape=pltpu.VMEM((128, 384), jnp.bfloat16),
        grid=(1,),
        in_specs=[SMEM] * 3 + [pl.BlockSpec((1, 128, 128), lambda i: (2, 0, 0))] + [VMEM] * len(after),
        out_specs=VMEM,
        cost_estimate=pl.CostEstimate(flops=10**11, transcendentals=0, bytes_accessed=10**5),
        compiler_params=pltpu.CompilerParams(vmem_limit_bytes=2 << 20),
        name="row_matrix",
    )(cosines, sines, hi, off_chip(gates), *map(on_chip, after))


def hold_kernel(in_ref, keep_partner, other, out_ref):
    out_ref[...] = in_ref[...]


def hold(left, *after):
    return pl.pallas_call(
        hold_kernel,
        out_shape=pltpu.VMEM(left.shape, left.dtype),
        in_specs=[VMEM] * (1 + len(after)),
        out_specs=VMEM,
        compiler_params=pltpu.CompilerParams(vmem_limit_bytes=2 << 20),
        cost_estimate=pl.CostEstimate(flops=10**11, transcendentals=0, bytes_accessed=10**5),
        name="hold",
    )(*map(on_chip, (left, *after)))


def write_rows(left, values, right, lines, out_ref):
    for s, value in enumerate(values):
        top, low = split(value)
        right[0:128, s * 128 : (s + 1) * 128] = top
        right[128:256, s * 128 : (s + 1) * 128] = low
    result = mm(left[:, 0:256], right[...]) + mm(left[:, 256:384], right[0:128, :])
    for s in range(8):
        lines[pl.ds(s, 128, stride=8), :] = result[:, s * 128 : (s + 1) * 128]
    out_ref[...] = lines[...].reshape(128, 1, 8, 128)


def joined(keep, other):
    return jnp.concatenate((keep[:, None], other[:, None]), 1).reshape(128, 128)


def rows_whole(left, own, *rest):
    out_ref, right, lines = rest[-3:]
    start = pl.program_id(0) * 8
    write_rows(left, [own[:, :, start + s].reshape(128, 128) for s in range(8)], right, lines, out_ref)


def rows_turning(cos_ref, sin_ref, lo_ref, left, keep, keep_partner, other, other_partner, *rest):
    out_ref, right, lines = rest[-3:]
    c, f = lo_turn(cos_ref, sin_ref, lo_ref)
    start = pl.program_id(0) * 8
    values = []
    for s in [start + i for i in range(8)]:
        values.append(joined(c * keep[:, s] + f * keep_partner[:, s], c * other[:, s] + f * other_partner[:, s]))
    write_rows(left, values, right, lines, out_ref)


def row_gate(body, scalars, left, parts, base, group):
    operands = [*scalars, on_chip(left), *map(on_chip, parts)]
    specs = [SMEM] * len(scalars) + [VMEM] * (1 + len(parts))
    aliases = {}
    if base is not None:
        aliases = {len(operands): 0}
        operands.append(base)
        specs.append(ANY)
    return pl.pallas_call(
        body,
        out_shape=jax.ShapeDtypeStruct((128, 4, 8, 128), jnp.float32),
        grid=(2,),
        in_specs=specs,
        out_specs=pl.BlockSpec((128, 1, 8, 128), lambda i: (0, group + i, 0, 0)),
        scratch_shapes=[pltpu.VMEM((256, 1024), jnp.bfloat16), pltpu.VMEM((1024, 128), jnp.float32)],
        input_output_aliases=aliases,
        compiler_params=pltpu.CompilerParams(vmem_limit_bytes=8 << 20),
        name="row_gate",
    )(*operands)


def swap_lo(value):
    count = lax.axis_size("lo")
    return lax.ppermute(value, "lo", [(i, i ^ count // 2) for i in range(count)])


def swap_hi(value):
    return lax.ppermute(value, "hi", [(i, i ^ 1) for i in range(lax.axis_size("hi"))])


def remap(value):
    count = lax.axis_size("hi")
    groups = [list(range(y, count, 2)) for y in range(2)]
    return lax.all_to_all(value, "hi", split_axis=0, concat_axis=0, tiled=True, axis_index_groups=groups)


def per_device(amplitudes, gates, angles, cz_pairs):
    hi = lax.axis_index("hi").reshape(1)
    lo = lax.axis_index("lo").reshape(1)
    cosines = jnp.cos(angles * 0.5)
    sines = jnp.sin(angles * 0.5)
    turn = (cosines, sines, lo)
    keep, send, upper, lower, late_left = local_gates(amplitudes.reshape(8, 2, 2, 128, 128), gates, cz_pairs, hi)
    other = swap_hi(send)
    keep_partner = swap_lo(keep)
    late = remap(late_gate(upper, lower, late_left))
    left = row_matrix(cosines, sines, hi, gates, keep_partner, other)
    early_parts = (keep, keep_partner, other, swap_lo(other))
    keep, send = cut(late, left)
    early = remap(merge(turn, early_parts, keep))
    other = swap_hi(send)
    keep_partner = swap_lo(keep)
    left = hold(left, keep_partner, other)
    result = row_gate(rows_turning, turn, left, (keep, keep_partner, other, swap_lo(other)), None, 2)
    result = row_gate(rows_whole, (), left, (early,), result, 0)
    return result.reshape(amplitudes.shape)


def solution(mesh):
    placed = (P("hi", "lo", None, None, None), P(), P(), P())
    return jax.shard_map(
        per_device,
        mesh=mesh,
        in_specs=placed,
        out_specs=P("hi", "lo", None, None, None),
        check_vma=False,
    )
```

```python
import jax
import jax.numpy as jnp
from jax import lax
from jax.experimental import pallas as pl
from jax.experimental.pallas import tpu as pltpu
from jax.sharding import PartitionSpec as P

QL = 14
QU = 5
QUBITS = QL + QU
STEP = 2
SMEM = pl.BlockSpec(memory_space=pltpu.SMEM)
VMEM = pl.BlockSpec(memory_space=pltpu.VMEM)
ANY = pl.BlockSpec(memory_space=pl.ANY)
BOTH = (8, 2, 16, 8, 128)
ONE = (8, 16, 8, 128)


def split(value):
    top = value.astype(jnp.bfloat16)
    return top, (value - top.astype(jnp.float32)).astype(jnp.bfloat16)


def fold_parity(bits):
    for step in (8, 4, 2, 1):
        bits = bits ^ (bits >> step)
    return bits & 1


def mm(left, right):
    return lax.dot_general(left, right, (((1,), (0,)), ((), ())), preferred_element_type=jnp.float32)


def on_chip(value):
    return pltpu.with_memory_space_constraint(value, pltpu.VMEM)


def off_chip(value):
    return pltpu.with_memory_space_constraint(value, pltpu.HBM)


def gate_pair(left, upper, lower):
    wide = mm(left[0], jnp.concatenate((upper, lower), 1))
    return wide[:, 0:256] + wide[:, 256:512] + mm(left[1], upper)


def local_kernel(cz_ref, hi_ref, x_ref, g_ref, *rest):
    keep_ref, send_ref, upper_ref, lower_ref, late_left_ref = rest[:5]
    adj, masks, flips, low_sign, right0, left1 = rest[5:]
    step = pl.program_id(0)
    odd = hi_ref[0] & 1

    @pl.when(step == 0)
    def _():
        for q in range(QUBITS):
            adj[q] = 0
        for p in range(cz_ref.shape[1]):
            a = cz_ref[0, p]
            b = cz_ref[1, p]
            q = jnp.maximum(a, b)
            adj[q] = adj[q] ^ (1 << jnp.minimum(a, b))
        masks[0] = 0
        flips[0] = 0
        for u in range(QU):
            row = adj[QL + u]
            for m in range(1 << u):
                masks[m + (1 << u)] = masks[m] ^ (row & ((1 << QL) - 1))
                flips[m + (1 << u)] = flips[m] ^ fold_parity((row >> QL) & m)
        row_id = lax.broadcasted_iota(jnp.int32, (128, 128), 0)
        lane_id = lax.broadcasted_iota(jnp.int32, (128, 128), 1)
        index = row_id * 128 + lane_id
        partner = jnp.zeros_like(index)
        for q in range(1, QL):
            partner = partner ^ jnp.where((index >> q & 1) == 1, adj[q], 0)
        low_sign[...] = 1.0 - 2.0 * fold_parity(index & partner).astype(jnp.float32)
        hi0, lo0 = split(g_ref[0].T)
        right0[0:128, 0:128] = hi0
        right0[0:128, 128:256] = lo0
        right0[128:256, 0:128] = hi0
        right0[128:256, 128:256] = jnp.zeros((128, 128), jnp.bfloat16)
        hi1, lo1 = split(g_ref[1])
        row = lax.broadcasted_iota(jnp.int32, (256, 128), 0)
        column = lax.broadcasted_iota(jnp.int32, (256, 128), 1)
        choose = jnp.where(column == (row & 3) * 32 + (row >> 3), 1.0, 0.0).astype(jnp.bfloat16)
        first = (row >> 2 & 1) == 0
        for i, part in enumerate((hi1, lo1)):
            picked = mm(choose, part)
            one = jnp.where(first, picked, 0.0).astype(jnp.bfloat16)
            other = jnp.where(first, 0.0, picked).astype(jnp.bfloat16)
            left1[i, :, 0:128] = one[0:128]
            left1[i, :, 128:256] = other[0:128]
            late_left_ref[i, :, 0:128] = one[128:256]
            late_left_ref[i, :, 128:256] = other[128:256]

    small = lax.broadcasted_iota(jnp.int32, (8, 128), 0) * 128 + lax.broadcasted_iota(jnp.int32, (8, 128), 1)
    for local in range(STEP):
        z = step * STEP + local
        tops = []
        lows = []
        for s in range(2):
            signed = []
            y = odd ^ s
            for r in range(2):
                m = z * 4 + y * 2 + r
                mask = masks[m]
                sign = 1.0 - 2.0 * (fold_parity(small & mask) ^ flips[m]).astype(jnp.float32)
                for q in range(10, QL):
                    flip = 1.0 - 2.0 * (mask >> q & 1).astype(jnp.float32)
                    sign = jnp.concatenate((sign, sign * flip), 0)
                signed.append(x_ref[local, y, r] * sign * low_sign[...])
            top, low = split(jnp.concatenate(signed, 0))
            both = mm(jnp.concatenate((top, low), 1), right0[...])
            top, low = split(both[:, 0:128] + both[:, 128:256])
            tops.append(top)
            lows.append(low)
        upper = jnp.concatenate(tops, 1)
        lower = jnp.concatenate(lows, 1)
        upper_ref[z] = upper
        lower_ref[z] = lower
        result = gate_pair(left1, upper, lower)
        keep_ref[z] = result[:, 0:128].reshape(16, 8, 128)
        send_ref[z] = result[:, 128:256].reshape(16, 8, 128)


def local_gates(x, gates, cz_pairs, hi):
    held = pltpu.VMEM((8, 256, 256), jnp.bfloat16)
    return pl.pallas_call(
        local_kernel,
        out_shape=[
            pltpu.VMEM(ONE, jnp.float32),
            pltpu.VMEM(ONE, jnp.float32),
            held,
            held,
            pltpu.VMEM((2, 128, 256), jnp.bfloat16),
        ],
        grid=(8 // STEP,),
        in_specs=[
            SMEM,
            SMEM,
            pl.BlockSpec((STEP, 2, 2, 128, 128), lambda i: (i, 0, 0, 0, 0)),
            pl.BlockSpec((3, 128, 128), lambda i: (0, 0, 0)),
        ],
        out_specs=[VMEM] * 5,
        scratch_shapes=[
            pltpu.SMEM((QUBITS,), jnp.int32),
            pltpu.SMEM((1 << QU,), jnp.int32),
            pltpu.SMEM((1 << QU,), jnp.int32),
            pltpu.VMEM((128, 128), jnp.float32),
            pltpu.VMEM((256, 256), jnp.bfloat16),
            pltpu.VMEM((2, 128, 256), jnp.bfloat16),
        ],
        compiler_params=pltpu.CompilerParams(vmem_limit_bytes=16 << 20),
        name="local_gates",
    )(cz_pairs.T, hi, off_chip(x), off_chip(gates))


def late_kernel(upper_ref, lower_ref, left_ref, late_ref):
    for z in range(8):
        result = gate_pair(left_ref, upper_ref[z], lower_ref[z])
        for s in range(2):
            late_ref[z, s] = result[:, s * 128 : (s + 1) * 128].reshape(16, 8, 128)


def late_gate(upper, lower, left):
    return pl.pallas_call(
        late_kernel,
        out_shape=jax.ShapeDtypeStruct(BOTH, jnp.float32),
        in_specs=[VMEM] * 3,
        out_specs=VMEM,
        compiler_params=pltpu.CompilerParams(vmem_limit_bytes=6 << 20),
        name="late_gate",
    )(on_chip(upper), on_chip(lower), on_chip(left))


def lo_turn(cos_ref, sin_ref, lo_ref):
    sine = sin_ref[0]
    return cos_ref[0], jnp.where((lo_ref[0] >> 4 & 1) == 1, sine, -sine)


def merge_kernel(cos_ref, sin_ref, lo_ref, keep, keep_partner, other, other_partner, late_keep, out_ref):
    c, f = lo_turn(cos_ref, sin_ref, lo_ref)
    out_ref[:, 0] = c * keep[...] + f * keep_partner[...]
    out_ref[:, 1] = c * other[...] + f * other_partner[...]


def merge(turn, parts, late_keep):
    return pl.pallas_call(
        merge_kernel,
        out_shape=jax.ShapeDtypeStruct(BOTH, jnp.float32),
        in_specs=[SMEM] * 3 + [VMEM] * 5,
        out_specs=VMEM,
        compiler_params=pltpu.CompilerParams(vmem_limit_bytes=4 << 20),
        name="merge",
    )(*turn, *map(on_chip, parts), on_chip(late_keep))


def cut_kernel(in_ref, left_ref, keep_ref, send_ref):
    keep_ref[...] = in_ref[:, 0]
    send_ref[...] = in_ref[:, 1]


def cut(value, left):
    return pl.pallas_call(
        cut_kernel,
        out_shape=[pltpu.VMEM(ONE, jnp.float32)] * 2,
        in_specs=[VMEM, VMEM],
        out_specs=[VMEM] * 2,
        compiler_params=pltpu.CompilerParams(vmem_limit_bytes=4 << 20),
        name="cut",
    )(on_chip(value), on_chip(left))


def matrix_kernel(cos_ref, sin_ref, hi_ref, g_ref, other, left_ref):
    gate = g_ref[0]
    lane = lax.broadcasted_iota(jnp.int32, (128, 128), 1)
    upper = (lane >> 3 & 1) == 1
    crossed = jnp.where(upper, pltpu.roll(gate, 8, 1), pltpu.roll(gate, 120, 1))
    cosine = cos_ref[1]
    sine = jnp.where(upper, -sin_ref[1], sin_ref[1])
    turned = jnp.where((hi_ref[0] & 1) == 1, cosine * crossed - sine * gate, cosine * gate + sine * crossed)
    top, low = split(turned)
    left_ref[:, 0:128] = top
    left_ref[:, 128:256] = top
    left_ref[:, 256:384] = low


def row_matrix(cosines, sines, hi, gates, *after):
    return pl.pallas_call(
        matrix_kernel,
        out_shape=pltpu.VMEM((128, 384), jnp.bfloat16),
        grid=(1,),
        in_specs=[SMEM] * 3 + [pl.BlockSpec((1, 128, 128), lambda i: (2, 0, 0))] + [VMEM] * len(after),
        out_specs=VMEM,
        cost_estimate=pl.CostEstimate(flops=15 * 10**9, transcendentals=0, bytes_accessed=10**5),
        compiler_params=pltpu.CompilerParams(vmem_limit_bytes=2 << 20),
        name="row_matrix",
    )(cosines, sines, hi, off_chip(gates), *map(on_chip, after))


def hold_kernel(in_ref, other, out_ref):
    out_ref[...] = in_ref[...]


def hold(left, *after):
    return pl.pallas_call(
        hold_kernel,
        out_shape=pltpu.VMEM(left.shape, left.dtype),
        in_specs=[VMEM] * (1 + len(after)),
        out_specs=VMEM,
        compiler_params=pltpu.CompilerParams(vmem_limit_bytes=2 << 20),
        cost_estimate=pl.CostEstimate(flops=15 * 10**9, transcendentals=0, bytes_accessed=10**5),
        name="hold",
    )(*map(on_chip, (left, *after)))


def write_rows(left, values, right, lines, out_ref):
    for s, value in enumerate(values):
        top, low = split(value)
        right[0:128, s * 128 : (s + 1) * 128] = top
        right[128:256, s * 128 : (s + 1) * 128] = low
    result = mm(left[:, 0:256], right[...]) + mm(left[:, 256:384], right[0:128, :])
    for s in range(8):
        lines[pl.ds(s, 128, stride=8), :] = result[:, s * 128 : (s + 1) * 128]
    out_ref[...] = lines[...].reshape(128, 1, 8, 128)


def joined(keep, other):
    return jnp.concatenate((keep[:, None], other[:, None]), 1).reshape(128, 128)


def rows_whole(left, own, *rest):
    out_ref, right, lines = rest[-3:]
    start = pl.program_id(0) * 8
    write_rows(left, [own[:, :, start + s].reshape(128, 128) for s in range(8)], right, lines, out_ref)


def rows_turning(cos_ref, sin_ref, lo_ref, left, keep, keep_partner, other, other_partner, *rest):
    out_ref, right, lines = rest[-3:]
    c, f = lo_turn(cos_ref, sin_ref, lo_ref)
    start = pl.program_id(0) * 8
    values = []
    for s in [start + i for i in range(8)]:
        values.append(joined(c * keep[:, s] + f * keep_partner[:, s], c * other[:, s] + f * other_partner[:, s]))
    write_rows(left, values, right, lines, out_ref)


def row_gate(body, scalars, left, parts, base, group):
    operands = [*scalars, on_chip(left), *map(on_chip, parts)]
    specs = [SMEM] * len(scalars) + [VMEM] * (1 + len(parts))
    aliases = {}
    if base is not None:
        aliases = {len(operands): 0}
        operands.append(base)
        specs.append(ANY)
    return pl.pallas_call(
        body,
        out_shape=jax.ShapeDtypeStruct((128, 4, 8, 128), jnp.float32),
        grid=(2,),
        in_specs=specs,
        out_specs=pl.BlockSpec((128, 1, 8, 128), lambda i: (0, group + i, 0, 0)),
        scratch_shapes=[pltpu.VMEM((256, 1024), jnp.bfloat16), pltpu.VMEM((1024, 128), jnp.float32)],
        input_output_aliases=aliases,
        compiler_params=pltpu.CompilerParams(vmem_limit_bytes=8 << 20),
        name="row_gate",
    )(*operands)


def swap_lo(value):
    count = lax.axis_size("lo")
    return lax.ppermute(value, "lo", [(i, i ^ count // 2) for i in range(count)])


def swap_hi(value):
    return lax.ppermute(value, "hi", [(i, i ^ 1) for i in range(lax.axis_size("hi"))])


def remap(value):
    count = lax.axis_size("hi")
    groups = [list(range(y, count, 2)) for y in range(2)]
    return lax.all_to_all(value, "hi", split_axis=0, concat_axis=0, tiled=True, axis_index_groups=groups)


def per_device(amplitudes, gates, angles, cz_pairs):
    hi = lax.axis_index("hi").reshape(1)
    lo = lax.axis_index("lo").reshape(1)
    cosines = jnp.cos(angles * 0.5)
    sines = jnp.sin(angles * 0.5)
    turn = (cosines, sines, lo)
    keep, send, upper, lower, late_left = local_gates(amplitudes.reshape(8, 2, 2, 128, 128), gates, cz_pairs, hi)
    other = swap_hi(send)
    keep_partner = swap_lo(keep)
    late = remap(late_gate(upper, lower, late_left))
    left = row_matrix(cosines, sines, hi, gates, other)
    early_parts = (keep, keep_partner, other, swap_lo(other))
    keep, send = cut(late, left)
    early = remap(merge(turn, early_parts, keep))
    other = swap_hi(send)
    keep_partner = swap_lo(keep)
    left = hold(left, other)
    result = row_gate(rows_whole, (), left, (early,), None, 0)
    result = row_gate(rows_turning, turn, left, (keep, keep_partner, other, swap_lo(other)), result, 2)
    return result.reshape(amplitudes.shape)


def solution(mesh):
    placed = (P("hi", "lo", None, None, None), P(), P(), P())
    return jax.shard_map(
        per_device,
        mesh=mesh,
        in_specs=placed,
        out_specs=P("hi", "lo", None, None, None),
        check_vma=False,
    )
```

```python
import jax
import jax.numpy as jnp
from jax import lax
from jax.experimental import pallas as pl
from jax.experimental.pallas import tpu as pltpu
from jax.sharding import PartitionSpec as P

QL = 14
QU = 5
QUBITS = QL + QU
STEP = 2
SMEM = pl.BlockSpec(memory_space=pltpu.SMEM)
VMEM = pl.BlockSpec(memory_space=pltpu.VMEM)
ANY = pl.BlockSpec(memory_space=pl.ANY)
BOTH = (8, 2, 16, 8, 128)
ONE = (8, 16, 8, 128)
PART = (8, 8, 8, 128)


def split(value):
    top = value.astype(jnp.bfloat16)
    return top, (value - top.astype(jnp.float32)).astype(jnp.bfloat16)


def fold_parity(bits):
    for step in (8, 4, 2, 1):
        bits = bits ^ (bits >> step)
    return bits & 1


def mm(left, right):
    return lax.dot_general(left, right, (((1,), (0,)), ((), ())), preferred_element_type=jnp.float32)


def on_chip(value):
    return pltpu.with_memory_space_constraint(value, pltpu.VMEM)


def off_chip(value):
    return pltpu.with_memory_space_constraint(value, pltpu.HBM)


def gate_pair(left, upper, lower):
    wide = mm(left[0], jnp.concatenate((upper, lower), 1))
    return wide[:, 0:256] + wide[:, 256:512] + mm(left[1], upper)


def local_kernel(cz_ref, hi_ref, x_ref, g_ref, *rest):
    keep_ref, send1_ref, send2_ref, upper_ref, lower_ref, late_left_ref = rest[:6]
    adj, masks, flips, low_sign, right0, left1 = rest[6:]
    step = pl.program_id(0)
    odd = hi_ref[0] & 1

    @pl.when(step == 0)
    def _():
        for q in range(QUBITS):
            adj[q] = 0
        for p in range(cz_ref.shape[1]):
            a = cz_ref[0, p]
            b = cz_ref[1, p]
            q = jnp.maximum(a, b)
            adj[q] = adj[q] ^ (1 << jnp.minimum(a, b))
        masks[0] = 0
        flips[0] = 0
        for u in range(QU):
            row = adj[QL + u]
            for m in range(1 << u):
                masks[m + (1 << u)] = masks[m] ^ (row & ((1 << QL) - 1))
                flips[m + (1 << u)] = flips[m] ^ fold_parity((row >> QL) & m)
        row_id = lax.broadcasted_iota(jnp.int32, (128, 128), 0)
        lane_id = lax.broadcasted_iota(jnp.int32, (128, 128), 1)
        index = row_id * 128 + lane_id
        partner = jnp.zeros_like(index)
        for q in range(1, QL):
            partner = partner ^ jnp.where((index >> q & 1) == 1, adj[q], 0)
        low_sign[...] = 1.0 - 2.0 * fold_parity(index & partner).astype(jnp.float32)
        hi0, lo0 = split(g_ref[0].T)
        right0[0:128, 0:128] = hi0
        right0[0:128, 128:256] = lo0
        right0[128:256, 0:128] = hi0
        right0[128:256, 128:256] = jnp.zeros((128, 128), jnp.bfloat16)
        hi1, lo1 = split(g_ref[1])
        row = lax.broadcasted_iota(jnp.int32, (256, 128), 0)
        column = lax.broadcasted_iota(jnp.int32, (256, 128), 1)
        choose = jnp.where(column == (row & 3) * 32 + (row >> 3), 1.0, 0.0).astype(jnp.bfloat16)
        first = (row >> 2 & 1) == 0
        for i, part in enumerate((hi1, lo1)):
            picked = mm(choose, part)
            one = jnp.where(first, picked, 0.0).astype(jnp.bfloat16)
            other = jnp.where(first, 0.0, picked).astype(jnp.bfloat16)
            left1[i, :, 0:128] = one[0:128]
            left1[i, :, 128:256] = other[0:128]
            late_left_ref[i, :, 0:128] = one[128:256]
            late_left_ref[i, :, 128:256] = other[128:256]

    small = lax.broadcasted_iota(jnp.int32, (8, 128), 0) * 128 + lax.broadcasted_iota(jnp.int32, (8, 128), 1)
    for local in range(STEP):
        z = step * STEP + local
        tops = []
        lows = []
        for s in range(2):
            signed = []
            y = odd ^ s
            for r in range(2):
                m = z * 4 + y * 2 + r
                mask = masks[m]
                sign = 1.0 - 2.0 * (fold_parity(small & mask) ^ flips[m]).astype(jnp.float32)
                for q in range(10, QL):
                    flip = 1.0 - 2.0 * (mask >> q & 1).astype(jnp.float32)
                    sign = jnp.concatenate((sign, sign * flip), 0)
                signed.append(x_ref[local, y, r] * sign * low_sign[...])
            top, low = split(jnp.concatenate(signed, 0))
            both = mm(jnp.concatenate((top, low), 1), right0[...])
            top, low = split(both[:, 0:128] + both[:, 128:256])
            tops.append(top)
            lows.append(low)
        upper = jnp.concatenate(tops, 1)
        lower = jnp.concatenate(lows, 1)
        upper_ref[z] = upper
        lower_ref[z] = lower
        result = gate_pair(left1, upper, lower)
        keep_ref[z] = result[:, 0:128].reshape(16, 8, 128)
        send1_ref[z] = result[0:64, 128:256].reshape(8, 8, 128)
        send2_ref[z] = result[64:128, 128:256].reshape(8, 8, 128)


def local_gates(x, gates, cz_pairs, hi):
    held = pltpu.VMEM((8, 256, 256), jnp.bfloat16)
    return pl.pallas_call(
        local_kernel,
        out_shape=[
            pltpu.VMEM(ONE, jnp.float32),
            pltpu.VMEM(PART, jnp.float32),
            pltpu.VMEM(PART, jnp.float32),
            held,
            held,
            pltpu.VMEM((2, 128, 256), jnp.bfloat16),
        ],
        grid=(8 // STEP,),
        in_specs=[
            SMEM,
            SMEM,
            pl.BlockSpec((STEP, 2, 2, 128, 128), lambda i: (i, 0, 0, 0, 0)),
            pl.BlockSpec((3, 128, 128), lambda i: (0, 0, 0)),
        ],
        out_specs=[VMEM] * 6,
        scratch_shapes=[
            pltpu.SMEM((QUBITS,), jnp.int32),
            pltpu.SMEM((1 << QU,), jnp.int32),
            pltpu.SMEM((1 << QU,), jnp.int32),
            pltpu.VMEM((128, 128), jnp.float32),
            pltpu.VMEM((256, 256), jnp.bfloat16),
            pltpu.VMEM((2, 128, 256), jnp.bfloat16),
        ],
        compiler_params=pltpu.CompilerParams(vmem_limit_bytes=16 << 20),
        name="local_gates",
    )(cz_pairs.T, hi, off_chip(x), off_chip(gates))


def late_kernel(upper_ref, lower_ref, left_ref, late_ref):
    for z in range(8):
        result = gate_pair(left_ref, upper_ref[z], lower_ref[z])
        for s in range(2):
            late_ref[z, s] = result[:, s * 128 : (s + 1) * 128].reshape(16, 8, 128)


def late_gate(upper, lower, left):
    return pl.pallas_call(
        late_kernel,
        out_shape=jax.ShapeDtypeStruct(BOTH, jnp.float32),
        in_specs=[VMEM] * 3,
        out_specs=VMEM,
        compiler_params=pltpu.CompilerParams(vmem_limit_bytes=6 << 20),
        name="late_gate",
    )(on_chip(upper), on_chip(lower), on_chip(left))


def lo_turn(cos_ref, sin_ref, lo_ref):
    sine = sin_ref[0]
    return cos_ref[0], jnp.where((lo_ref[0] >> 4 & 1) == 1, sine, -sine)


def turn_kernel(cos_ref, sin_ref, lo_ref, own_ref, partner_ref, out_ref):
    c, f = lo_turn(cos_ref, sin_ref, lo_ref)
    out_ref[...] = c * own_ref[...] + f * partner_ref[...]


def turn_part(turn, own):
    return pl.pallas_call(
        turn_kernel,
        out_shape=pltpu.VMEM(own.shape, own.dtype),
        in_specs=[SMEM] * 3 + [VMEM] * 2,
        out_specs=VMEM,
        compiler_params=pltpu.CompilerParams(vmem_limit_bytes=2 << 20),
        name="turn_part",
    )(*turn, on_chip(own), on_chip(swap_lo(own)))


def merge_kernel(cos_ref, sin_ref, lo_ref, keep, keep_partner, first, first_partner, second, *rest):
    out_ref = rest[-1]
    c, f = lo_turn(cos_ref, sin_ref, lo_ref)
    out_ref[:, 0] = c * keep[...] + f * keep_partner[...]
    out_ref[:, 1, 0:8] = c * first[...] + f * first_partner[...]
    out_ref[:, 1, 8:16] = second[...]


def merge(turn, parts, after):
    return pl.pallas_call(
        merge_kernel,
        out_shape=jax.ShapeDtypeStruct(BOTH, jnp.float32),
        in_specs=[SMEM] * 3 + [VMEM] * (5 + len(after)),
        out_specs=VMEM,
        compiler_params=pltpu.CompilerParams(vmem_limit_bytes=4 << 20),
        name="merge",
    )(*turn, *map(on_chip, (*parts, *after)))


def cut_kernel(in_ref, *rest):
    keep_ref, first_ref, second_ref, sems = rest[-4:]
    copies = [
        pltpu.make_async_copy(in_ref.at[:, 1, pl.ds(8, 8)], second_ref, sems.at[0]),
        pltpu.make_async_copy(in_ref.at[:, 1, pl.ds(0, 8)], first_ref, sems.at[1]),
        pltpu.make_async_copy(in_ref.at[:, 0], keep_ref, sems.at[2]),
    ]
    for copy in copies:
        copy.start()
    for copy in copies:
        copy.wait()


def cut(value, after):
    return pl.pallas_call(
        cut_kernel,
        out_shape=[pltpu.VMEM(ONE, jnp.float32), pltpu.VMEM(PART, jnp.float32), pltpu.VMEM(PART, jnp.float32)],
        in_specs=[ANY] + [VMEM] * len(after),
        out_specs=[VMEM] * 3,
        scratch_shapes=[pltpu.SemaphoreType.DMA((3,))],
        compiler_params=pltpu.CompilerParams(vmem_limit_bytes=4 << 20),
        name="cut",
    )(off_chip(value), *map(on_chip, after))


def matrix_kernel(cos_ref, sin_ref, hi_ref, g_ref, *rest):
    left_ref = rest[-1]
    gate = g_ref[0]
    lane = lax.broadcasted_iota(jnp.int32, (128, 128), 1)
    upper = (lane >> 3 & 1) == 1
    crossed = jnp.where(upper, pltpu.roll(gate, 8, 1), pltpu.roll(gate, 120, 1))
    cosine = cos_ref[1]
    sine = jnp.where(upper, -sin_ref[1], sin_ref[1])
    turned = jnp.where((hi_ref[0] & 1) == 1, cosine * crossed - sine * gate, cosine * gate + sine * crossed)
    top, low = split(turned)
    left_ref[:, 0:128] = top
    left_ref[:, 128:256] = top
    left_ref[:, 256:384] = low


def row_matrix(cosines, sines, hi, gates, *after):
    return pl.pallas_call(
        matrix_kernel,
        out_shape=pltpu.VMEM((128, 384), jnp.bfloat16),
        grid=(1,),
        in_specs=[SMEM] * 3 + [pl.BlockSpec((1, 128, 128), lambda i: (2, 0, 0))] + [VMEM] * len(after),
        out_specs=VMEM,
        cost_estimate=pl.CostEstimate(flops=10**6, transcendentals=0, bytes_accessed=10**5),
        compiler_params=pltpu.CompilerParams(vmem_limit_bytes=2 << 20),
        name="row_matrix",
    )(cosines, sines, hi, off_chip(gates), *map(on_chip, after))


def hold_kernel(in_ref, *rest):
    rest[-1][...] = in_ref[...]


def hold(left, *after):
    return pl.pallas_call(
        hold_kernel,
        out_shape=pltpu.VMEM(left.shape, left.dtype),
        in_specs=[VMEM] * (1 + len(after)),
        out_specs=VMEM,
        compiler_params=pltpu.CompilerParams(vmem_limit_bytes=2 << 20),
        cost_estimate=pl.CostEstimate(flops=10**11, transcendentals=0, bytes_accessed=10**5),
        name="hold",
    )(*map(on_chip, (left, *after)))


def write_rows(left, values, right, lines, out_ref):
    for s, value in enumerate(values):
        top, low = split(value)
        right[0:128, s * 128 : (s + 1) * 128] = top
        right[128:256, s * 128 : (s + 1) * 128] = low
    result = mm(left[:, 0:256], right[...]) + mm(left[:, 256:384], right[0:128, :])
    for s in range(8):
        lines[pl.ds(s, 128, stride=8), :] = result[:, s * 128 : (s + 1) * 128]
    out_ref[...] = lines[...].reshape(128, 1, 8, 128)


def joined(keep, other):
    return jnp.concatenate((keep[:, None], other[:, None]), 1).reshape(128, 128)


def rows_whole(left, own, *rest):
    out_ref, right, lines = rest[-3:]
    start = pl.program_id(0) * 8
    write_rows(left, [own[:, :, start + s].reshape(128, 128) for s in range(8)], right, lines, out_ref)


def rows_turning(cos_ref, sin_ref, lo_ref, left, keep, keep_partner, first, first_partner, second, *rest):
    out_ref, right, lines = rest[-3:]
    c, f = lo_turn(cos_ref, sin_ref, lo_ref)
    for group in range(2):

        @pl.when(pl.program_id(0) == group)
        def _():
            values = []
            for s in range(8):
                j = group * 8 + s
                other = second[:, s] if group else c * first[:, s] + f * first_partner[:, s]
                values.append(joined(c * keep[:, j] + f * keep_partner[:, j], other))
            write_rows(left, values, right, lines, out_ref)


def row_gate(body, scalars, left, parts, base, group):
    operands = [*scalars, on_chip(left), *map(on_chip, parts)]
    specs = [SMEM] * len(scalars) + [VMEM] * (1 + len(parts))
    aliases = {}
    if base is not None:
        aliases = {len(operands): 0}
        operands.append(base)
        specs.append(ANY)
    return pl.pallas_call(
        body,
        out_shape=jax.ShapeDtypeStruct((128, 4, 8, 128), jnp.float32),
        grid=(2,),
        in_specs=specs,
        out_specs=pl.BlockSpec((128, 1, 8, 128), lambda i: (0, group + i, 0, 0)),
        scratch_shapes=[pltpu.VMEM((256, 1024), jnp.bfloat16), pltpu.VMEM((1024, 128), jnp.float32)],
        input_output_aliases=aliases,
        compiler_params=pltpu.CompilerParams(vmem_limit_bytes=8 << 20),
        name="row_gate",
    )(*operands)


def swap_lo(value):
    count = lax.axis_size("lo")
    return lax.ppermute(value, "lo", [(i, i ^ count // 2) for i in range(count)])


def swap_hi(value):
    return lax.ppermute(value, "hi", [(i, i ^ 1) for i in range(lax.axis_size("hi"))])


def remap(value):
    count = lax.axis_size("hi")
    groups = [list(range(y, count, 2)) for y in range(2)]
    return lax.all_to_all(value, "hi", split_axis=0, concat_axis=0, tiled=True, axis_index_groups=groups)


def cross(turn, keep, first, second):
    first_other = swap_hi(first)
    second = turn_part(turn, second)
    return (keep, swap_lo(keep), first_other, swap_lo(first_other), swap_hi(second)), second


def per_device(amplitudes, gates, angles, cz_pairs):
    hi = lax.axis_index("hi").reshape(1)
    lo = lax.axis_index("lo").reshape(1)
    cosines = jnp.cos(angles * 0.5)
    sines = jnp.sin(angles * 0.5)
    turn = (cosines, sines, lo)
    keep, first, second, upper, lower, late_left = local_gates(
        amplitudes.reshape(8, 2, 2, 128, 128), gates, cz_pairs, hi
    )
    late = remap(late_gate(upper, lower, late_left))
    early_parts, turned = cross(turn, keep, first, second)
    left = row_matrix(cosines, sines, hi, gates)
    late_keep, late_first, late_second = cut(late, (left, early_parts[3]))
    early = remap(merge(turn, early_parts, (late_first,)))
    late_parts, late_turned = cross(turn, late_keep, late_first, late_second)
    left = hold(left, late_parts[2], late_turned)
    result = row_gate(rows_turning, turn, left, late_parts, None, 2)
    result = row_gate(rows_whole, (), left, (early,), result, 0)
    return result.reshape(amplitudes.shape)


def solution(mesh):
    placed = (P("hi", "lo", None, None, None), P(), P(), P())
    return jax.shard_map(
        per_device,
        mesh=mesh,
        in_specs=placed,
        out_specs=P("hi", "lo", None, None, None),
        check_vma=False,
    )
```

```python
import jax
import jax.numpy as jnp
from jax import lax
from jax.experimental import pallas as pl
from jax.experimental.pallas import tpu as pltpu
from jax.sharding import PartitionSpec as P

QL = 14
QU = 5
QUBITS = QL + QU
STEP = 4
SMEM = pl.BlockSpec(memory_space=pltpu.SMEM)
VMEM = pl.BlockSpec(memory_space=pltpu.VMEM)
ANY = pl.BlockSpec(memory_space=pl.ANY)
BOTH = (8, 2, 16, 8, 128)
ONE = (8, 16, 8, 128)
PART = (8, 8, 8, 128)


def split(value):
    top = value.astype(jnp.bfloat16)
    return top, (value - top.astype(jnp.float32)).astype(jnp.bfloat16)


def fold_parity(bits):
    for step in (8, 4, 2, 1):
        bits = bits ^ (bits >> step)
    return bits & 1


def mm(left, right):
    return lax.dot_general(left, right, (((1,), (0,)), ((), ())), preferred_element_type=jnp.float32)


def on_chip(value):
    return pltpu.with_memory_space_constraint(value, pltpu.VMEM)


def off_chip(value):
    return pltpu.with_memory_space_constraint(value, pltpu.HBM)


def gate_pair(left, upper, lower):
    wide = mm(left[0], jnp.concatenate((upper, lower), 1))
    return wide[:, 0:256] + wide[:, 256:512] + mm(left[1], upper)


def local_kernel(cz_ref, hi_ref, x_ref, g_ref, *rest):
    keep_ref, send1_ref, send2_ref, late_ref = rest[:4]
    adj, masks, flips, low_sign, right0, left1 = rest[4:]
    step = pl.program_id(0)
    odd = hi_ref[0] & 1

    @pl.when(step == 0)
    def _():
        for q in range(QUBITS):
            adj[q] = 0
        for p in range(cz_ref.shape[1]):
            a = cz_ref[0, p]
            b = cz_ref[1, p]
            q = jnp.maximum(a, b)
            adj[q] = adj[q] ^ (1 << jnp.minimum(a, b))
        masks[0] = 0
        flips[0] = 0
        for u in range(QU):
            row = adj[QL + u]
            for m in range(1 << u):
                masks[m + (1 << u)] = masks[m] ^ (row & ((1 << QL) - 1))
                flips[m + (1 << u)] = flips[m] ^ fold_parity((row >> QL) & m)
        row_id = lax.broadcasted_iota(jnp.int32, (128, 128), 0)
        lane_id = lax.broadcasted_iota(jnp.int32, (128, 128), 1)
        index = row_id * 128 + lane_id
        partner = jnp.zeros_like(index)
        for q in range(1, QL):
            partner = partner ^ jnp.where((index >> q & 1) == 1, adj[q], 0)
        low_sign[...] = 1.0 - 2.0 * fold_parity(index & partner).astype(jnp.float32)
        hi0, lo0 = split(g_ref[0].T)
        right0[0:128, 0:128] = hi0
        right0[0:128, 128:256] = lo0
        right0[128:256, 0:128] = hi0
        right0[128:256, 128:256] = jnp.zeros((128, 128), jnp.bfloat16)
        hi1, lo1 = split(g_ref[1])
        row = lax.broadcasted_iota(jnp.int32, (256, 128), 0)
        column = lax.broadcasted_iota(jnp.int32, (256, 128), 1)
        choose = jnp.where(column == (row & 3) * 32 + (row >> 3), 1.0, 0.0).astype(jnp.bfloat16)
        first = (row >> 2 & 1) == 0
        for i, part in enumerate((hi1, lo1)):
            picked = mm(choose, part)
            one = jnp.where(first, picked, 0.0).astype(jnp.bfloat16)
            other = jnp.where(first, 0.0, picked).astype(jnp.bfloat16)
            left1[i, :, 0:128] = one
            left1[i, :, 128:256] = other

    small = lax.broadcasted_iota(jnp.int32, (8, 128), 0) * 128 + lax.broadcasted_iota(jnp.int32, (8, 128), 1)
    for local in range(STEP):
        z = step * STEP + local
        tops = []
        lows = []
        for s in range(2):
            signed = []
            y = odd ^ s
            for r in range(2):
                m = z * 4 + y * 2 + r
                mask = masks[m]
                sign = 1.0 - 2.0 * (fold_parity(small & mask) ^ flips[m]).astype(jnp.float32)
                for q in range(10, QL):
                    flip = 1.0 - 2.0 * (mask >> q & 1).astype(jnp.float32)
                    sign = jnp.concatenate((sign, sign * flip), 0)
                signed.append(x_ref[local, y, r] * sign * low_sign[...])
            top, low = split(jnp.concatenate(signed, 0))
            both = mm(jnp.concatenate((top, low), 1), right0[...])
            top, low = split(both[:, 0:128] + both[:, 128:256])
            tops.append(top)
            lows.append(low)
        upper = jnp.concatenate(tops, 1)
        lower = jnp.concatenate(lows, 1)
        result = gate_pair(left1, upper, lower)
        keep_ref[z] = result[0:128, 0:128].reshape(16, 8, 128)
        send1_ref[z] = result[0:64, 128:256].reshape(8, 8, 128)
        send2_ref[z] = result[64:128, 128:256].reshape(8, 8, 128)
        for s in range(2):
            late_ref[local, s] = result[128:256, s * 128 : (s + 1) * 128].reshape(16, 8, 128)


def local_gates(x, gates, cz_pairs, hi):
    return pl.pallas_call(
        local_kernel,
        out_shape=[
            pltpu.VMEM(ONE, jnp.float32),
            pltpu.VMEM(PART, jnp.float32),
            pltpu.VMEM(PART, jnp.float32),
            jax.ShapeDtypeStruct(BOTH, jnp.float32),
        ],
        grid=(8 // STEP,),
        in_specs=[
            SMEM,
            SMEM,
            pl.BlockSpec((STEP, 2, 2, 128, 128), lambda i: (i, 0, 0, 0, 0)),
            pl.BlockSpec((3, 128, 128), lambda i: (0, 0, 0)),
        ],
        out_specs=[VMEM] * 3 + [pl.BlockSpec((STEP, 2, 16, 8, 128), lambda i: (i, 0, 0, 0, 0))],
        scratch_shapes=[
            pltpu.SMEM((QUBITS,), jnp.int32),
            pltpu.SMEM((1 << QU,), jnp.int32),
            pltpu.SMEM((1 << QU,), jnp.int32),
            pltpu.VMEM((128, 128), jnp.float32),
            pltpu.VMEM((256, 256), jnp.bfloat16),
            pltpu.VMEM((2, 256, 256), jnp.bfloat16),
        ],
        compiler_params=pltpu.CompilerParams(vmem_limit_bytes=16 << 20),
        name="local_gates",
    )(off_chip(cz_pairs.T), hi, off_chip(x), off_chip(gates))


def lo_turn(cos_ref, sin_ref, lo_ref):
    sine = sin_ref[0]
    return cos_ref[0], jnp.where((lo_ref[0] >> 4 & 1) == 1, sine, -sine)


def turn_kernel(cos_ref, sin_ref, lo_ref, own_ref, partner_ref, out_ref):
    c, f = lo_turn(cos_ref, sin_ref, lo_ref)
    out_ref[...] = c * own_ref[...] + f * partner_ref[...]


def turn_part(turn, own):
    return pl.pallas_call(
        turn_kernel,
        out_shape=pltpu.VMEM(own.shape, own.dtype),
        in_specs=[SMEM] * 3 + [VMEM] * 2,
        out_specs=VMEM,
        compiler_params=pltpu.CompilerParams(vmem_limit_bytes=2 << 20),
        name="turn_part",
    )(*turn, on_chip(own), on_chip(swap_lo(own)))


def merge_kernel(cos_ref, sin_ref, lo_ref, keep, keep_partner, first, first_partner, second, *rest):
    out_ref = rest[-1]
    c, f = lo_turn(cos_ref, sin_ref, lo_ref)
    out_ref[:, 0] = c * keep[...] + f * keep_partner[...]
    out_ref[:, 1, 0:8] = c * first[...] + f * first_partner[...]
    out_ref[:, 1, 8:16] = second[...]


def merge(turn, parts, after):
    return pl.pallas_call(
        merge_kernel,
        out_shape=jax.ShapeDtypeStruct(BOTH, jnp.float32),
        in_specs=[SMEM] * 3 + [VMEM] * (5 + len(after)),
        out_specs=VMEM,
        compiler_params=pltpu.CompilerParams(vmem_limit_bytes=4 << 20),
        name="merge",
    )(*turn, *map(on_chip, (*parts, *after)))


def cut_kernel(in_ref, *rest):
    keep_ref, first_ref, second_ref, sems = rest[-4:]
    copies = [
        pltpu.make_async_copy(in_ref.at[:, 1, pl.ds(8, 8)], second_ref, sems.at[0]),
        pltpu.make_async_copy(in_ref.at[:, 1, pl.ds(0, 8)], first_ref, sems.at[1]),
        pltpu.make_async_copy(in_ref.at[:, 0], keep_ref, sems.at[2]),
    ]
    for copy in copies:
        copy.start()
    for copy in copies:
        copy.wait()


def cut(value, after):
    return pl.pallas_call(
        cut_kernel,
        out_shape=[pltpu.VMEM(ONE, jnp.float32), pltpu.VMEM(PART, jnp.float32), pltpu.VMEM(PART, jnp.float32)],
        in_specs=[ANY] + [VMEM] * len(after),
        out_specs=[VMEM] * 3,
        scratch_shapes=[pltpu.SemaphoreType.DMA((3,))],
        compiler_params=pltpu.CompilerParams(vmem_limit_bytes=4 << 20),
        name="cut",
    )(off_chip(value), *map(on_chip, after))


def matrix_kernel(cos_ref, sin_ref, hi_ref, g_ref, *rest):
    left_ref = rest[-1]
    gate = g_ref[0]
    lane = lax.broadcasted_iota(jnp.int32, (128, 128), 1)
    upper = (lane >> 3 & 1) == 1
    crossed = jnp.where(upper, pltpu.roll(gate, 8, 1), pltpu.roll(gate, 120, 1))
    cosine = cos_ref[1]
    sine = jnp.where(upper, -sin_ref[1], sin_ref[1])
    turned = jnp.where((hi_ref[0] & 1) == 1, cosine * crossed - sine * gate, cosine * gate + sine * crossed)
    top, low = split(turned)
    left_ref[:, 0:128] = top
    left_ref[:, 128:256] = top
    left_ref[:, 256:384] = low


def row_matrix(cosines, sines, hi, gates, *after):
    return pl.pallas_call(
        matrix_kernel,
        out_shape=pltpu.VMEM((128, 384), jnp.bfloat16),
        grid=(1,),
        in_specs=[SMEM] * 3 + [pl.BlockSpec((1, 128, 128), lambda i: (2, 0, 0))] + [VMEM] * len(after),
        out_specs=VMEM,
        cost_estimate=pl.CostEstimate(flops=10**11, transcendentals=0, bytes_accessed=10**5),
        compiler_params=pltpu.CompilerParams(vmem_limit_bytes=2 << 20),
        name="row_matrix",
    )(cosines, sines, hi, off_chip(gates), *map(on_chip, after))


def write_rows(left, values, right, lines, out_ref):
    for s, value in enumerate(values):
        top, low = split(value)
        right[0:128, s * 128 : (s + 1) * 128] = top
        right[128:256, s * 128 : (s + 1) * 128] = low
    result = mm(left[:, 0:256], right[...]) + mm(left[:, 256:384], right[0:128, :])
    for s in range(8):
        lines[pl.ds(s, 128, stride=8), :] = result[:, s * 128 : (s + 1) * 128]
    out_ref[...] = lines[...].reshape(128, 1, 8, 128)


def joined(keep, other):
    return jnp.concatenate((keep[:, None], other[:, None]), 1).reshape(128, 128)


def rows_whole(left, own, *rest):
    out_ref, right, lines = rest[-3:]
    start = pl.program_id(0) * 8
    write_rows(left, [own[:, :, start + s].reshape(128, 128) for s in range(8)], right, lines, out_ref)


def rows_turning(cos_ref, sin_ref, lo_ref, left, keep, keep_partner, first, first_partner, second, *rest):
    out_ref, right, lines = rest[-3:]
    c, f = lo_turn(cos_ref, sin_ref, lo_ref)
    for group in range(2):

        @pl.when(pl.program_id(0) == group)
        def _():
            values = []
            for s in range(8):
                j = group * 8 + s
                other = second[:, s] if group else c * first[:, s] + f * first_partner[:, s]
                values.append(joined(c * keep[:, j] + f * keep_partner[:, j], other))
            write_rows(left, values, right, lines, out_ref)


def row_gate(body, scalars, left, parts, base, group):
    operands = [*scalars, on_chip(left), *map(on_chip, parts)]
    specs = [SMEM] * len(scalars) + [VMEM] * (1 + len(parts))
    aliases = {}
    if base is not None:
        aliases = {len(operands): 0}
        operands.append(base)
        specs.append(ANY)
    return pl.pallas_call(
        body,
        out_shape=jax.ShapeDtypeStruct((128, 4, 8, 128), jnp.float32),
        grid=(2,),
        in_specs=specs,
        out_specs=pl.BlockSpec((128, 1, 8, 128), lambda i: (0, group + i, 0, 0)),
        scratch_shapes=[pltpu.VMEM((256, 1024), jnp.bfloat16), pltpu.VMEM((1024, 128), jnp.float32)],
        input_output_aliases=aliases,
        compiler_params=pltpu.CompilerParams(vmem_limit_bytes=8 << 20),
        name="row_gate",
    )(*operands)


def swap_lo(value):
    count = lax.axis_size("lo")
    return lax.ppermute(value, "lo", [(i, i ^ count // 2) for i in range(count)])


def swap_hi(value):
    return lax.ppermute(value, "hi", [(i, i ^ 1) for i in range(lax.axis_size("hi"))])


def remap(value):
    count = lax.axis_size("hi")
    groups = [list(range(y, count, 2)) for y in range(2)]
    return lax.all_to_all(value, "hi", split_axis=0, concat_axis=0, tiled=True, axis_index_groups=groups)


def cross(turn, keep, first, second):
    first_other = swap_hi(first)
    second = turn_part(turn, second)
    return (keep, swap_lo(keep), first_other, swap_lo(first_other), swap_hi(second)), second


def per_device(amplitudes, gates, angles, cz_pairs):
    hi = lax.axis_index("hi").reshape(1)
    lo = lax.axis_index("lo").reshape(1)
    cosines = jnp.cos(angles * 0.5)
    sines = jnp.sin(angles * 0.5)
    turn = (cosines, sines, lo)
    keep, first, second, late = local_gates(
        amplitudes.reshape(8, 2, 2, 128, 128), gates, cz_pairs, hi
    )
    late = remap(late)
    early_parts, turned = cross(turn, keep, first, second)
    late_keep, late_first, late_second = cut(late, (early_parts[3],))
    early = remap(merge(turn, early_parts, (late_first,)))
    late_parts, late_turned = cross(turn, late_keep, late_first, late_second)
    left = row_matrix(cosines, sines, hi, gates, late_parts[2], late_turned)
    result = row_gate(rows_turning, turn, left, late_parts, None, 2)
    result = row_gate(rows_whole, (), left, (early,), result, 0)
    return result.reshape(amplitudes.shape)


def solution(mesh):
    placed = (P("hi", "lo", None, None, None), P(), P(), P())
    return jax.shard_map(
        per_device,
        mesh=mesh,
        in_specs=placed,
        out_specs=P("hi", "lo", None, None, None),
        check_vma=False,
    )
```

```python
import jax
import jax.numpy as jnp
from jax import lax
from jax.experimental import pallas as pl
from jax.experimental.pallas import tpu as pltpu
from jax.sharding import PartitionSpec as P

QL = 14
QU = 5
QUBITS = QL + QU
STEP = 4
SMEM = pl.BlockSpec(memory_space=pltpu.SMEM)
VMEM = pl.BlockSpec(memory_space=pltpu.VMEM)
ANY = pl.BlockSpec(memory_space=pl.ANY)
BOTH = (8, 2, 16, 8, 128)
ONE = (8, 16, 8, 128)
PART = (8, 8, 8, 128)


def split(value):
    top = value.astype(jnp.bfloat16)
    return top, (value - top.astype(jnp.float32)).astype(jnp.bfloat16)


def fold_parity(bits):
    for step in (8, 4, 2, 1):
        bits = bits ^ (bits >> step)
    return bits & 1


def mm(left, right):
    return lax.dot_general(left, right, (((1,), (0,)), ((), ())), preferred_element_type=jnp.float32)


def on_chip(value):
    return pltpu.with_memory_space_constraint(value, pltpu.VMEM)


def off_chip(value):
    return pltpu.with_memory_space_constraint(value, pltpu.HBM)


def gate_pair(left, upper, lower):
    wide = mm(left[0], jnp.concatenate((upper, lower), 1))
    return wide[:, 0:256] + wide[:, 256:512] + mm(left[1], upper)


def local_kernel(cz_ref, hi_ref, x_ref, g_ref, *rest):
    keep_ref, send1_ref, send2_ref, late_ref = rest[:4]
    adj, masks, flips, low_sign, right0, left1 = rest[4:]
    step = pl.program_id(0)
    odd = hi_ref[0] & 1

    @pl.when(step == 0)
    def _():
        for q in range(QUBITS):
            adj[q] = 0
        for p in range(cz_ref.shape[1]):
            a = cz_ref[0, p]
            b = cz_ref[1, p]
            q = jnp.maximum(a, b)
            adj[q] = adj[q] ^ (1 << jnp.minimum(a, b))
        masks[0] = 0
        flips[0] = 0
        for u in range(QU):
            row = adj[QL + u]
            for m in range(1 << u):
                masks[m + (1 << u)] = masks[m] ^ (row & ((1 << QL) - 1))
                flips[m + (1 << u)] = flips[m] ^ fold_parity((row >> QL) & m)
        row_id = lax.broadcasted_iota(jnp.int32, (128, 128), 0)
        lane_id = lax.broadcasted_iota(jnp.int32, (128, 128), 1)
        index = row_id * 128 + lane_id
        partner = jnp.zeros_like(index)
        for q in range(1, QL):
            partner = partner ^ jnp.where((index >> q & 1) == 1, adj[q], 0)
        low_sign[...] = 1.0 - 2.0 * fold_parity(index & partner).astype(jnp.float32)
        hi0, lo0 = split(g_ref[0].T)
        right0[0:128, 0:128] = hi0
        right0[0:128, 128:256] = lo0
        right0[128:256, 0:128] = hi0
        right0[128:256, 128:256] = jnp.zeros((128, 128), jnp.bfloat16)
        hi1, lo1 = split(g_ref[1])
        row = lax.broadcasted_iota(jnp.int32, (256, 128), 0)
        column = lax.broadcasted_iota(jnp.int32, (256, 128), 1)
        choose = jnp.where(column == (row & 3) * 32 + (row >> 3), 1.0, 0.0).astype(jnp.bfloat16)
        first = (row >> 2 & 1) == 0
        for i, part in enumerate((hi1, lo1)):
            picked = mm(choose, part)
            one = jnp.where(first, picked, 0.0).astype(jnp.bfloat16)
            other = jnp.where(first, 0.0, picked).astype(jnp.bfloat16)
            left1[i, :, 0:128] = one
            left1[i, :, 128:256] = other

    small = lax.broadcasted_iota(jnp.int32, (8, 128), 0) * 128 + lax.broadcasted_iota(jnp.int32, (8, 128), 1)
    for local in range(STEP):
        z = step * STEP + local
        tops = []
        lows = []
        for s in range(2):
            signed = []
            y = odd ^ s
            for r in range(2):
                m = z * 4 + y * 2 + r
                mask = masks[m]
                sign = 1.0 - 2.0 * (fold_parity(small & mask) ^ flips[m]).astype(jnp.float32)
                for q in range(10, QL):
                    flip = 1.0 - 2.0 * (mask >> q & 1).astype(jnp.float32)
                    sign = jnp.concatenate((sign, sign * flip), 0)
                signed.append(x_ref[local, y, r] * sign * low_sign[...])
            top, low = split(jnp.concatenate(signed, 0))
            both = mm(jnp.concatenate((top, low), 1), right0[...])
            top, low = split(both[:, 0:128] + both[:, 128:256])
            tops.append(top)
            lows.append(low)
        upper = jnp.concatenate(tops, 1)
        lower = jnp.concatenate(lows, 1)
        result = gate_pair(left1, upper, lower)
        keep_ref[z] = result[0:128, 0:128].reshape(16, 8, 128)
        send1_ref[z] = result[0:64, 128:256].reshape(8, 8, 128)
        send2_ref[z] = result[64:128, 128:256].reshape(8, 8, 128)
        for s in range(2):
            late_ref[local, s] = result[128:256, s * 128 : (s + 1) * 128].reshape(16, 8, 128)


def local_gates(x, gates, cz_pairs, hi):
    return pl.pallas_call(
        local_kernel,
        out_shape=[
            pltpu.VMEM(ONE, jnp.float32),
            pltpu.VMEM(PART, jnp.float32),
            pltpu.VMEM(PART, jnp.float32),
            jax.ShapeDtypeStruct(BOTH, jnp.float32),
        ],
        grid=(8 // STEP,),
        in_specs=[
            SMEM,
            SMEM,
            pl.BlockSpec((STEP, 2, 2, 128, 128), lambda i: (i, 0, 0, 0, 0)),
            pl.BlockSpec((3, 128, 128), lambda i: (0, 0, 0)),
        ],
        out_specs=[VMEM] * 3 + [pl.BlockSpec((STEP, 2, 16, 8, 128), lambda i: (i, 0, 0, 0, 0))],
        scratch_shapes=[
            pltpu.SMEM((QUBITS,), jnp.int32),
            pltpu.SMEM((1 << QU,), jnp.int32),
            pltpu.SMEM((1 << QU,), jnp.int32),
            pltpu.VMEM((128, 128), jnp.float32),
            pltpu.VMEM((256, 256), jnp.bfloat16),
            pltpu.VMEM((2, 256, 256), jnp.bfloat16),
        ],
        compiler_params=pltpu.CompilerParams(vmem_limit_bytes=16 << 20),
        name="local_gates",
    )(off_chip(cz_pairs.T), hi, off_chip(x), off_chip(gates))


def lo_turn(cos_ref, sin_ref, lo_ref):
    sine = sin_ref[0]
    return cos_ref[0], jnp.where((lo_ref[0] >> 4 & 1) == 1, sine, -sine)


def turn_kernel(cos_ref, sin_ref, lo_ref, own_ref, partner_ref, out_ref):
    c, f = lo_turn(cos_ref, sin_ref, lo_ref)
    out_ref[...] = c * own_ref[...] + f * partner_ref[...]


def turn_part(turn, own):
    return pl.pallas_call(
        turn_kernel,
        out_shape=pltpu.VMEM(own.shape, own.dtype),
        in_specs=[SMEM] * 3 + [VMEM] * 2,
        out_specs=VMEM,
        compiler_params=pltpu.CompilerParams(vmem_limit_bytes=2 << 20),
        name="turn_part",
    )(*turn, on_chip(own), on_chip(swap_lo(own)))


def merge_kernel(cos_ref, sin_ref, lo_ref, keep, keep_partner, first, first_partner, second, *rest):
    out_ref = rest[-1]
    c, f = lo_turn(cos_ref, sin_ref, lo_ref)
    out_ref[:, 0] = c * keep[...] + f * keep_partner[...]
    out_ref[:, 1, 0:8] = c * first[...] + f * first_partner[...]
    out_ref[:, 1, 8:16] = second[...]


def merge(turn, parts, after):
    return pl.pallas_call(
        merge_kernel,
        out_shape=jax.ShapeDtypeStruct(BOTH, jnp.float32),
        in_specs=[SMEM] * 3 + [VMEM] * (5 + len(after)),
        out_specs=VMEM,
        compiler_params=pltpu.CompilerParams(vmem_limit_bytes=4 << 20),
        name="merge",
    )(*turn, *map(on_chip, (*parts, *after)))


def cut_kernel(in_ref, *rest):
    keep_ref, first_ref, second_ref, sems = rest[-4:]
    copies = [
        pltpu.make_async_copy(in_ref.at[:, 1, pl.ds(8, 8)], second_ref, sems.at[0]),
        pltpu.make_async_copy(in_ref.at[:, 1, pl.ds(0, 8)], first_ref, sems.at[1]),
        pltpu.make_async_copy(in_ref.at[:, 0], keep_ref, sems.at[2]),
    ]
    for copy in copies:
        copy.start()
    for copy in copies:
        copy.wait()


def cut(value, after):
    return pl.pallas_call(
        cut_kernel,
        out_shape=[pltpu.VMEM(ONE, jnp.float32), pltpu.VMEM(PART, jnp.float32), pltpu.VMEM(PART, jnp.float32)],
        in_specs=[ANY] + [VMEM] * len(after),
        out_specs=[VMEM] * 3,
        scratch_shapes=[pltpu.SemaphoreType.DMA((3,))],
        compiler_params=pltpu.CompilerParams(vmem_limit_bytes=4 << 20),
        name="cut",
    )(off_chip(value), *map(on_chip, after))


def matrix_kernel(cos_ref, sin_ref, hi_ref, g_ref, *rest):
    left_ref = rest[-1]
    gate = g_ref[0]
    lane = lax.broadcasted_iota(jnp.int32, (128, 128), 1)
    upper = (lane >> 3 & 1) == 1
    crossed = jnp.where(upper, pltpu.roll(gate, 8, 1), pltpu.roll(gate, 120, 1))
    cosine = cos_ref[1]
    sine = jnp.where(upper, -sin_ref[1], sin_ref[1])
    turned = jnp.where((hi_ref[0] & 1) == 1, cosine * crossed - sine * gate, cosine * gate + sine * crossed)
    top, low = split(turned)
    left_ref[:, 0:128] = top
    left_ref[:, 128:256] = top
    left_ref[:, 256:384] = low


def row_matrix(cosines, sines, hi, gates, *after):
    return pl.pallas_call(
        matrix_kernel,
        out_shape=pltpu.VMEM((128, 384), jnp.bfloat16),
        grid=(1,),
        in_specs=[SMEM] * 3 + [pl.BlockSpec((1, 128, 128), lambda i: (2, 0, 0))] + [VMEM] * len(after),
        out_specs=VMEM,
        cost_estimate=pl.CostEstimate(flops=10**11, transcendentals=0, bytes_accessed=10**5),
        compiler_params=pltpu.CompilerParams(vmem_limit_bytes=2 << 20),
        name="row_matrix",
    )(cosines, sines, hi, off_chip(gates), *map(on_chip, after))


def write_rows(left, values, right, lines, out_ref):
    for s, value in enumerate(values):
        top, low = split(value)
        right[0:128, s * 128 : (s + 1) * 128] = top
        right[128:256, s * 128 : (s + 1) * 128] = low
    result = mm(left[:, 0:256], right[...]) + mm(left[:, 256:384], right[0:128, :])
    for s in range(8):
        lines[pl.ds(s, 128, stride=8), :] = result[:, s * 128 : (s + 1) * 128]
    out_ref[...] = lines[0:1024].reshape(128, 1, 8, 128)


def joined(keep, other):
    return jnp.concatenate((keep[:, None], other[:, None]), 1).reshape(128, 128)


def rows_whole(left, own, *rest):
    out_ref, right, lines = rest[-3:]
    start = pl.program_id(0) * 8
    write_rows(left, [own[:, :, start + s].reshape(128, 128) for s in range(8)], right, lines, out_ref)


def rows_turning(cos_ref, sin_ref, lo_ref, left, keep, keep_partner, first, first_partner, second, *rest):
    out_ref, right, lines = rest[-3:]
    c, f = lo_turn(cos_ref, sin_ref, lo_ref)
    for group in range(2):

        @pl.when(pl.program_id(0) == group)
        def _():
            values = []
            for s in range(8):
                j = group * 8 + s
                other = second[:, s] if group else c * first[:, s] + f * first_partner[:, s]
                values.append(joined(c * keep[:, j] + f * keep_partner[:, j], other))
            write_rows(left, values, right, lines, out_ref)


def row_gate(body, scalars, left, parts, base, group):
    operands = [*scalars, on_chip(left), *map(on_chip, parts)]
    specs = [SMEM] * len(scalars) + [VMEM] * (1 + len(parts))
    aliases = {}
    if base is not None:
        aliases = {len(operands): 0}
        operands.append(base)
        specs.append(ANY)
    return pl.pallas_call(
        body,
        out_shape=jax.ShapeDtypeStruct((128, 4, 8, 128), jnp.float32),
        grid=(2,),
        in_specs=specs,
        out_specs=pl.BlockSpec((128, 1, 8, 128), lambda i: (0, group + i, 0, 0)),
        scratch_shapes=[pltpu.VMEM((256, 1024), jnp.bfloat16), pltpu.VMEM((1040, 128), jnp.float32)],
        input_output_aliases=aliases,
        compiler_params=pltpu.CompilerParams(vmem_limit_bytes=8 << 20),
        name="row_gate",
    )(*operands)


def swap_lo(value):
    count = lax.axis_size("lo")
    return lax.ppermute(value, "lo", [(i, i ^ count // 2) for i in range(count)])


def swap_hi(value):
    return lax.ppermute(value, "hi", [(i, i ^ 1) for i in range(lax.axis_size("hi"))])


def remap(value):
    count = lax.axis_size("hi")
    groups = [list(range(y, count, 2)) for y in range(2)]
    return lax.all_to_all(value, "hi", split_axis=0, concat_axis=0, tiled=True, axis_index_groups=groups)


def cross(turn, keep, first, second):
    first_other = swap_hi(first)
    second = turn_part(turn, second)
    return (keep, swap_lo(keep), first_other, swap_lo(first_other), swap_hi(second)), second


def per_device(amplitudes, gates, angles, cz_pairs):
    hi = lax.axis_index("hi").reshape(1)
    lo = lax.axis_index("lo").reshape(1)
    cosines = jnp.cos(angles * 0.5)
    sines = jnp.sin(angles * 0.5)
    turn = (cosines, sines, lo)
    keep, first, second, late = local_gates(
        amplitudes.reshape(8, 2, 2, 128, 128), gates, cz_pairs, hi
    )
    late = remap(late)
    early_parts, turned = cross(turn, keep, first, second)
    late_keep, late_first, late_second = cut(late, (early_parts[3], turned))
    early = remap(merge(turn, early_parts, (late_first,)))
    late_parts, late_turned = cross(turn, late_keep, late_first, late_second)
    left = row_matrix(cosines, sines, hi, gates, late_parts[2], late_turned)
    result = row_gate(rows_turning, turn, left, late_parts, None, 2)
    result = row_gate(rows_whole, (), left, (early,), result, 0)
    return result.reshape(amplitudes.shape)


def solution(mesh):
    placed = (P("hi", "lo", None, None, None), P(), P(), P())
    return jax.shard_map(
        per_device,
        mesh=mesh,
        in_specs=placed,
        out_specs=P("hi", "lo", None, None, None),
        check_vma=False,
    )
```

```python
import jax
import jax.numpy as jnp
from jax import lax
from jax.experimental import pallas as pl
from jax.experimental.pallas import tpu as pltpu
from jax.sharding import PartitionSpec as P

QL = 14
QU = 5
QUBITS = QL + QU
STEP = 8
SMEM = pl.BlockSpec(memory_space=pltpu.SMEM)
VMEM = pl.BlockSpec(memory_space=pltpu.VMEM)
ANY = pl.BlockSpec(memory_space=pl.ANY)
BOTH = (8, 2, 16, 8, 128)
ONE = (8, 16, 8, 128)
PART = (8, 8, 8, 128)


def split(value):
    top = value.astype(jnp.bfloat16)
    return top, (value - top.astype(jnp.float32)).astype(jnp.bfloat16)


def fold_parity(bits):
    for step in (8, 4, 2, 1):
        bits = bits ^ (bits >> step)
    return bits & 1


def mm(left, right):
    return lax.dot_general(left, right, (((1,), (0,)), ((), ())), preferred_element_type=jnp.float32)


def on_chip(value):
    return pltpu.with_memory_space_constraint(value, pltpu.VMEM)


def off_chip(value):
    return pltpu.with_memory_space_constraint(value, pltpu.HBM)


def gate_pair(left, upper, lower):
    wide = mm(left[0], jnp.concatenate((upper, lower), 1))
    return wide[:, 0:256] + wide[:, 256:512] + mm(left[1], upper)


def local_kernel(cz_ref, hi_ref, x_ref, g_ref, *rest):
    keep_ref, send1_ref, send2_ref, late_ref = rest[:4]
    adj, masks, flips, low_sign, right0, left1 = rest[4:]
    step = pl.program_id(0)
    odd = hi_ref[0] & 1

    @pl.when(step == 0)
    def _():
        for q in range(QUBITS):
            adj[q] = 0
        for p in range(cz_ref.shape[1]):
            a = cz_ref[0, p]
            b = cz_ref[1, p]
            q = jnp.maximum(a, b)
            adj[q] = adj[q] ^ (1 << jnp.minimum(a, b))
        masks[0] = 0
        flips[0] = 0
        for u in range(QU):
            row = adj[QL + u]
            for m in range(1 << u):
                masks[m + (1 << u)] = masks[m] ^ (row & ((1 << QL) - 1))
                flips[m + (1 << u)] = flips[m] ^ fold_parity((row >> QL) & m)
        row_id = lax.broadcasted_iota(jnp.int32, (128, 128), 0)
        lane_id = lax.broadcasted_iota(jnp.int32, (128, 128), 1)
        index = row_id * 128 + lane_id
        partner = jnp.zeros_like(index)
        for q in range(1, QL):
            partner = partner ^ jnp.where((index >> q & 1) == 1, adj[q], 0)
        low_sign[...] = 1.0 - 2.0 * fold_parity(index & partner).astype(jnp.float32)
        hi0, lo0 = split(g_ref[0].T)
        right0[0:128, 0:128] = hi0
        right0[0:128, 128:256] = lo0
        right0[128:256, 0:128] = hi0
        right0[128:256, 128:256] = jnp.zeros((128, 128), jnp.bfloat16)
        hi1, lo1 = split(g_ref[1])
        row = lax.broadcasted_iota(jnp.int32, (256, 128), 0)
        column = lax.broadcasted_iota(jnp.int32, (256, 128), 1)
        choose = jnp.where(column == (row & 3) * 32 + (row >> 3), 1.0, 0.0).astype(jnp.bfloat16)
        first = (row >> 2 & 1) == 0
        for i, part in enumerate((hi1, lo1)):
            picked = mm(choose, part)
            one = jnp.where(first, picked, 0.0).astype(jnp.bfloat16)
            other = jnp.where(first, 0.0, picked).astype(jnp.bfloat16)
            left1[i, :, 0:128] = one
            left1[i, :, 128:256] = other

    small = lax.broadcasted_iota(jnp.int32, (8, 128), 0) * 128 + lax.broadcasted_iota(jnp.int32, (8, 128), 1)
    for local in range(STEP):
        z = step * STEP + local
        tops = []
        lows = []
        for s in range(2):
            signed = []
            y = odd ^ s
            for r in range(2):
                m = z * 4 + y * 2 + r
                mask = masks[m]
                sign = 1.0 - 2.0 * (fold_parity(small & mask) ^ flips[m]).astype(jnp.float32)
                for q in range(10, QL):
                    flip = 1.0 - 2.0 * (mask >> q & 1).astype(jnp.float32)
                    sign = jnp.concatenate((sign, sign * flip), 0)
                signed.append(x_ref[local, y, r] * sign * low_sign[...])
            top, low = split(jnp.concatenate(signed, 0))
            both = mm(jnp.concatenate((top, low), 1), right0[...])
            top, low = split(both[:, 0:128] + both[:, 128:256])
            tops.append(top)
            lows.append(low)
        upper = jnp.concatenate(tops, 1)
        lower = jnp.concatenate(lows, 1)
        result = gate_pair(left1, upper, lower)
        keep_ref[z] = result[0:128, 0:128].reshape(16, 8, 128)
        send1_ref[z] = result[0:64, 128:256].reshape(8, 8, 128)
        send2_ref[z] = result[64:128, 128:256].reshape(8, 8, 128)
        for s in range(2):
            late_ref[local, s] = result[128:256, s * 128 : (s + 1) * 128].reshape(16, 8, 128)


def local_gates(x, gates, cz_pairs, hi):
    return pl.pallas_call(
        local_kernel,
        out_shape=[
            pltpu.VMEM(ONE, jnp.float32),
            pltpu.VMEM(PART, jnp.float32),
            pltpu.VMEM(PART, jnp.float32),
            jax.ShapeDtypeStruct(BOTH, jnp.float32),
        ],
        grid=(8 // STEP,),
        in_specs=[
            SMEM,
            SMEM,
            pl.BlockSpec((STEP, 2, 2, 128, 128), lambda i: (i, 0, 0, 0, 0)),
            pl.BlockSpec((3, 128, 128), lambda i: (0, 0, 0)),
        ],
        out_specs=[VMEM] * 3 + [pl.BlockSpec((STEP, 2, 16, 8, 128), lambda i: (i, 0, 0, 0, 0))],
        scratch_shapes=[
            pltpu.SMEM((QUBITS,), jnp.int32),
            pltpu.SMEM((1 << QU,), jnp.int32),
            pltpu.SMEM((1 << QU,), jnp.int32),
            pltpu.VMEM((128, 128), jnp.float32),
            pltpu.VMEM((256, 256), jnp.bfloat16),
            pltpu.VMEM((2, 256, 256), jnp.bfloat16),
        ],
        compiler_params=pltpu.CompilerParams(vmem_limit_bytes=16 << 20),
        name="local_gates",
    )(off_chip(cz_pairs.T), hi, off_chip(x), off_chip(gates))


def lo_turn(cos_ref, sin_ref, lo_ref):
    sine = sin_ref[0]
    return cos_ref[0], jnp.where((lo_ref[0] >> 4 & 1) == 1, sine, -sine)


def turn_kernel(cos_ref, sin_ref, lo_ref, own_ref, partner_ref, out_ref):
    c, f = lo_turn(cos_ref, sin_ref, lo_ref)
    out_ref[...] = c * own_ref[...] + f * partner_ref[...]


def turn_part(turn, own):
    return pl.pallas_call(
        turn_kernel,
        out_shape=pltpu.VMEM(own.shape, own.dtype),
        in_specs=[SMEM] * 3 + [VMEM] * 2,
        out_specs=VMEM,
        compiler_params=pltpu.CompilerParams(vmem_limit_bytes=2 << 20),
        name="turn_part",
    )(*turn, on_chip(own), on_chip(swap_lo(own)))


def merge_kernel(cos_ref, sin_ref, lo_ref, keep, keep_partner, first, first_partner, second, *rest):
    out_ref = rest[-1]
    c, f = lo_turn(cos_ref, sin_ref, lo_ref)
    out_ref[:, 0] = c * keep[...] + f * keep_partner[...]
    out_ref[:, 1, 0:8] = c * first[...] + f * first_partner[...]
    out_ref[:, 1, 8:16] = second[...]


def merge(turn, parts, after):
    return pl.pallas_call(
        merge_kernel,
        out_shape=jax.ShapeDtypeStruct(BOTH, jnp.float32),
        in_specs=[SMEM] * 3 + [VMEM] * (5 + len(after)),
        out_specs=VMEM,
        compiler_params=pltpu.CompilerParams(vmem_limit_bytes=4 << 20),
        name="merge",
    )(*turn, *map(on_chip, (*parts, *after)))


def cut_kernel(in_ref, *rest):
    keep_ref, first_ref, second_ref, sems = rest[-4:]
    copies = [
        pltpu.make_async_copy(in_ref.at[:, 1, pl.ds(8, 8)], second_ref, sems.at[0]),
        pltpu.make_async_copy(in_ref.at[:, 1, pl.ds(0, 8)], first_ref, sems.at[1]),
        pltpu.make_async_copy(in_ref.at[:, 0], keep_ref, sems.at[2]),
    ]
    for copy in copies:
        copy.start()
    for copy in copies:
        copy.wait()


def cut(value, after):
    return pl.pallas_call(
        cut_kernel,
        out_shape=[pltpu.VMEM(ONE, jnp.float32), pltpu.VMEM(PART, jnp.float32), pltpu.VMEM(PART, jnp.float32)],
        in_specs=[ANY] + [VMEM] * len(after),
        out_specs=[VMEM] * 3,
        scratch_shapes=[pltpu.SemaphoreType.DMA((3,))],
        compiler_params=pltpu.CompilerParams(vmem_limit_bytes=4 << 20),
        name="cut",
    )(off_chip(value), *map(on_chip, after))


def matrix_kernel(cos_ref, sin_ref, hi_ref, g_ref, *rest):
    left_ref = rest[-1]
    gate = g_ref[0]
    lane = lax.broadcasted_iota(jnp.int32, (128, 128), 1)
    upper = (lane >> 3 & 1) == 1
    crossed = jnp.where(upper, pltpu.roll(gate, 8, 1), pltpu.roll(gate, 120, 1))
    cosine = cos_ref[1]
    sine = jnp.where(upper, -sin_ref[1], sin_ref[1])
    turned = jnp.where((hi_ref[0] & 1) == 1, cosine * crossed - sine * gate, cosine * gate + sine * crossed)
    top, low = split(turned)
    left_ref[:, 0:128] = top
    left_ref[:, 128:256] = top
    left_ref[:, 256:384] = low


def row_matrix(cosines, sines, hi, gates, *after):
    return pl.pallas_call(
        matrix_kernel,
        out_shape=pltpu.VMEM((128, 384), jnp.bfloat16),
        grid=(1,),
        in_specs=[SMEM] * 3 + [pl.BlockSpec((1, 128, 128), lambda i: (2, 0, 0))] + [VMEM] * len(after),
        out_specs=VMEM,
        cost_estimate=pl.CostEstimate(flops=10**11, transcendentals=0, bytes_accessed=10**5),
        compiler_params=pltpu.CompilerParams(vmem_limit_bytes=2 << 20),
        name="row_matrix",
    )(cosines, sines, hi, off_chip(gates), *map(on_chip, after))


def write_rows(left, values, right, lines, out_ref):
    for s, value in enumerate(values):
        top, low = split(value)
        right[0:128, s * 128 : (s + 1) * 128] = top
        right[128:256, s * 128 : (s + 1) * 128] = low
    result = mm(left[:, 0:256], right[...]) + mm(left[:, 256:384], right[0:128, :])
    for s in range(8):
        lines[pl.ds(s, 128, stride=8), :] = result[:, s * 128 : (s + 1) * 128]
    out_ref[...] = lines[...].reshape(128, 1, 8, 128)


def joined(keep, other):
    return jnp.concatenate((keep[:, None], other[:, None]), 1).reshape(128, 128)


def rows_whole(left, own, *rest):
    out_ref, right, lines = rest[-3:]
    start = pl.program_id(0) * 8
    write_rows(left, [own[:, :, start + s].reshape(128, 128) for s in range(8)], right, lines, out_ref)


def rows_turning(cos_ref, sin_ref, lo_ref, left, keep, keep_partner, first, first_partner, second, *rest):
    out_ref, right, lines = rest[-3:]
    c, f = lo_turn(cos_ref, sin_ref, lo_ref)
    for group in range(2):

        @pl.when(pl.program_id(0) == group)
        def _():
            values = []
            for s in range(8):
                j = group * 8 + s
                other = second[:, s] if group else c * first[:, s] + f * first_partner[:, s]
                values.append(joined(c * keep[:, j] + f * keep_partner[:, j], other))
            write_rows(left, values, right, lines, out_ref)


def row_gate(body, scalars, left, parts, base, group):
    operands = [*scalars, on_chip(left), *map(on_chip, parts)]
    specs = [SMEM] * len(scalars) + [VMEM] * (1 + len(parts))
    aliases = {}
    if base is not None:
        aliases = {len(operands): 0}
        operands.append(base)
        specs.append(ANY)
    return pl.pallas_call(
        body,
        out_shape=jax.ShapeDtypeStruct((128, 4, 8, 128), jnp.float32),
        grid=(2,),
        in_specs=specs,
        out_specs=pl.BlockSpec((128, 1, 8, 128), lambda i: (0, group + i, 0, 0)),
        scratch_shapes=[pltpu.VMEM((256, 1024), jnp.bfloat16), pltpu.VMEM((1024, 128), jnp.float32)],
        input_output_aliases=aliases,
        compiler_params=pltpu.CompilerParams(vmem_limit_bytes=8 << 20),
        name="row_gate",
    )(*operands)


def swap_lo(value):
    count = lax.axis_size("lo")
    return lax.ppermute(value, "lo", [(i, i ^ count // 2) for i in range(count)])


def swap_hi(value):
    return lax.ppermute(value, "hi", [(i, i ^ 1) for i in range(lax.axis_size("hi"))])


def remap(value):
    count = lax.axis_size("hi")
    groups = [list(range(y, count, 2)) for y in range(2)]
    return lax.all_to_all(value, "hi", split_axis=0, concat_axis=0, tiled=True, axis_index_groups=groups)


def cross(turn, keep, first, second):
    first_other = swap_hi(first)
    second = turn_part(turn, second)
    return (keep, swap_lo(keep), first_other, swap_lo(first_other), swap_hi(second)), second


def per_device(amplitudes, gates, angles, cz_pairs):
    hi = lax.axis_index("hi").reshape(1)
    lo = lax.axis_index("lo").reshape(1)
    cosines = jnp.cos(angles * 0.5)
    sines = jnp.sin(angles * 0.5)
    turn = (cosines, sines, lo)
    keep, first, second, late = local_gates(
        amplitudes.reshape(8, 2, 2, 128, 128), gates, cz_pairs, hi
    )
    late = remap(late)
    early_parts, turned = cross(turn, keep, first, second)
    late_keep, late_first, late_second = cut(late, (early_parts[3],))
    early = remap(merge(turn, early_parts, (late_first,)))
    late_parts, late_turned = cross(turn, late_keep, late_first, late_second)
    left = row_matrix(cosines, sines, hi, gates, late_parts[2], late_turned)
    result = row_gate(rows_turning, turn, left, late_parts, None, 2)
    result = row_gate(rows_whole, (), left, (early,), result, 0)
    return result.reshape(amplitudes.shape)


def solution(mesh):
    placed = (P("hi", "lo", None, None, None), P(), P(), P())
    return jax.shard_map(
        per_device,
        mesh=mesh,
        in_specs=placed,
        out_specs=P("hi", "lo", None, None, None),
        check_vma=False,
    )
```
